256 devices in a mesh: role: 2 (over core), dev: 64 (over x_hi, y, z), head: 2 (over x_lo).
Axes of the slice: x: 4 (x_hi: 2, x_lo: 2; x = x_hi * 2 + x_lo), y: 4, z: 8, core: 2. Of those that a mesh axis runs over, the one named last changes fastest.
Arguments:
- hidden: bfloat16 [2048, 4096], P(('role', 'dev', 'head')), may hold values from -6 to 6
- queries: bfloat16 [2048, 64, 128], P(('role', 'dev'), 'head'), as said below
- cache_keys: bfloat16 [2048, 128, 4, 128], P(('role', 'dev'), None, 'head'), as said below
- cache_values: bfloat16 [2048, 128, 4, 128], P(('role', 'dev'), None, 'head'), may hold values from -6 to 6
- new_keys: bfloat16 [2048, 4, 128], P(('role', 'dev'), 'head'), may hold values from -6 to 6
- new_values: bfloat16 [2048, 4, 128], P(('role', 'dev'), 'head'), may hold values from -6 to 6
- lengths: int32 [2048], P(('role', 'dev')), may hold values from 32 to 128, as said below
- out_proj: bfloat16 [8192, 4096], P('head', 'dev'), may hold values from -0.5 to 0.5
- norm_gain: float32 [4096], replicated, may hold values from 0.1 to 1.9
- expert_gate: bfloat16 [128, 4096, 768], P(('role', 'dev'), None, 'head'), may hold values from -0.09375 to 0.09375
- expert_up: bfloat16 [128, 4096, 768], P(('role', 'dev'), None, 'head'), may hold values from -0.09375 to 0.09375
- expert_down: bfloat16 [128, 768, 4096], P(('role', 'dev'), 'head'), may hold values from -0.21875 to 0.21875
- expert_ids: int32 [2048, 8], P(('role', 'dev', 'head')), may hold values from 0 to 127, all different within a row; in each aligned block of 8 rows (0 to 7, 8 to 15, ...) at most 2 rows name the same one
- gate_levels: int32 [2048, 8], P(('role', 'dev', 'head')), may hold values from 1 to 255
Outputs:
- layer_out: bfloat16 [2048, 4096], P(('role', 'dev', 'head'))
The draws below stay inside these ranges and needn't reach their ends.
Inputs may be any that keep to these rules, and one draw needn't show every extreme that they name: `queries`: query vectors of the new tokens. `cache_keys`: cached keys of the requests. `lengths`: the first request of each block of 16 rows holds 128 positions and the second holds 32. `expert_ids`: each row names 8 different experts; among the 8 rows of one device no expert is named more than 2 times, a bound that some block reaches.
All inputs are finite; a program needn't handle non-finite values.
Results may differ from the reference program's by a relative error of at most 0.0065.
Values may be sent and summed in bfloat16 or wider, within the bound.
No kernel may reach another device: no remote copies, remote signals or barrier semaphores. Data moves between devices by JAX's collectives and lax.ppermute only.
A program may use at most 64 MiB of HBM per device.

```python
import math
import jax
import jax.numpy as jnp
import numpy as np
from jax import lax

D = 4096
QH = 64
KVH = 4
HD = 128
TOPK = 8
FF = 768
CACHE = 128
R_DEV = 16
TOK_DEV = 8
ROWS = 2048
EXPERTS = 128
CAP = 2


def key_field(key):
    sampled = jax.random.normal(jax.random.fold_in(key, 31), (ROWS, CACHE, KVH, HD), jnp.float32)
    return sampled


def draw_cache_keys(key, part):
    return key_field(key).astype(jnp.bfloat16)


def draw_queries(key, part):
    sampled = jax.random.normal(jax.random.fold_in(key, 32), (ROWS, QH, HD), jnp.float32)
    return sampled.astype(jnp.bfloat16)


def draw_lengths(key, part):
    drawn = jax.random.randint(jax.random.fold_in(key, 41), (ROWS,), CACHE // 4, CACHE + 1, jnp.int32)
    position = jnp.arange(ROWS, dtype=jnp.int32) % R_DEV
    drawn = jnp.where(position == 0, CACHE, drawn)
    drawn = jnp.where(position == 1, CACHE // 4, drawn)
    return drawn.astype(jnp.int32)


def with_ends(values, rng, low, high):
    place = [jax.random.randint(jax.random.fold_in(rng, axis), (), 0, length) for axis, length in enumerate(values.shape)]
    longest = values.shape.index(max(values.shape))
    beside = place[:longest] + [(place[longest] + 1) % values.shape[longest]] + place[longest + 1:]
    return values.at[tuple(place)].set(low).at[tuple(beside)].set(high)


def steps_of(key, extent, shards, smallest, high):
    level, own = 1.0, jax.random.fold_in(key, 6)
    for axis_at, shards_of in shards:
        steps = jnp.exp(jax.random.uniform(jax.random.fold_in(own, axis_at), (shards_of,), jnp.float32, smallest / len(shards), high / len(shards)))
        level = level * jnp.repeat(steps, extent[axis_at] // shards_of).reshape([-1 if axis == axis_at else 1 for axis in range(len(extent))])
    return level


def shared_out(rng, own, number, rows, count, top, most, skew):
    order = jax.random.permutation(rng, count)
    heavy_load, usual = load_shares(count, rows * top, most, skew, True), load_shares(count, rows * top, most, skew, False)
    places = jnp.arange(count)

    def named(sizes, turn):
        used = int((sizes > 0).sum())
        fixed = max(1, used // 4)
        passed = fixed + (places - fixed + turn * (used - fixed)) % max(1, count - fixed)
        return jnp.zeros((count,), jnp.int32).at[order[jnp.where(places < fixed, places, passed)]].set(jnp.asarray(sizes, jnp.int32))

    sizes = jnp.where(number % 4 == 0, named(heavy_load, number // 4), named(usual, number - number // 4 - 1))
    mixed = jax.random.permutation(jax.random.fold_in(own, 3), count)
    giver, receiver = mixed[0:count // 2 * 2:2], mixed[1:count // 2 * 2:2]
    slack = jnp.minimum(sizes[giver] - 1, most - sizes[receiver]) // 2
    slack = jnp.where((giver == order[0]) | (receiver == order[0]) | (sizes[receiver] == 0), 0, jnp.maximum(slack, 0))
    passed = jax.random.randint(jax.random.fold_in(own, 4), (count // 2,), 0, 1 << 20) % (slack + 1)
    sizes = sizes.at[giver].add(-passed).at[receiver].add(passed)
    items = jnp.searchsorted(jnp.cumsum(sizes), jnp.arange(rows * top), side="right").astype(jnp.int32)
    table = items.reshape(top, rows).T
    table = table[jax.random.permutation(jax.random.fold_in(own, 1), rows)]
    turn = jax.random.randint(jax.random.fold_in(own, 2), (rows, 1), 0, top)
    return jnp.take_along_axis(table, (jnp.arange(top)[None, :] + turn) % top, axis=1)


def load_shares(amount, total, bound, skew, full):
    weights = [(1 << 20) // math.isqrt(rank ** skew) + 1 for rank in range(1, amount + 1)]
    largest = bound if full else min(bound, max(-(-total // amount), total * weights[0] // sum(weights)))
    least = 1 if total - largest >= amount - 1 else 0
    counts, spare = [largest] + [least] * (amount - 1), total - largest - least * (amount - 1)
    while spare > 0:
        movable = [i for i in range(1, amount) if counts[i] < largest] or [i for i in range(1, amount) if counts[i] < bound]
        whole, remaining = sum([weights[i] for i in movable]), spare
        for i in movable:
            addition = min(bound - counts[i], max(1, remaining * weights[i] // whole), spare)
            counts[i] = counts[i] + addition
            spare = spare - addition
    return np.array(counts)


def normal_values(stream_key, extent, scale, bound, shards=(), held_as=jnp.bfloat16):
    gain = steps_of(stream_key, extent, shards, -0.22, 0.18) if shards else 1.0
    result = jax.random.normal(stream_key, extent, jnp.float32) * scale * gain
    return jnp.minimum(jnp.maximum(result, -bound), bound).astype(held_as)


def setup_inputs(seed: int = 0) -> dict:
    key_list = jax.random.split(jax.random.key(seed), 15)
    hidden = normal_values(key_list[0], (ROWS, D), 1.0, 6.0, ((0, 256),))
    queries = draw_queries(jax.random.fold_in(key_list[14], 71), 0)
    cache_keys = draw_cache_keys(jax.random.fold_in(key_list[14], 71), 0)
    cache_values = normal_values(key_list[3], (ROWS, CACHE, KVH, HD), 1.0, 6.0, ((0, 128), (2, 2)))
    new_keys = normal_values(key_list[4], (ROWS, KVH, HD), 1.0, 6.0, ((0, 128), (1, 2)))
    new_values = normal_values(key_list[5], (ROWS, KVH, HD), 1.0, 6.0, ((0, 128), (1, 2)))
    lengths = draw_lengths(jax.random.fold_in(key_list[14], 71), 0)
    out_proj = normal_values(key_list[7], (QH * HD, D), HD ** -0.5, 0.5, ((0, 2), (1, 64)))
    norm_gain = jnp.clip(1.0 + 0.18 * jax.random.normal(key_list[8], (D,), jnp.float32), 0.1, 1.9)
    expert_gate = normal_values(key_list[9], (EXPERTS, D, FF), D ** -0.5, 0.09375, ((0, 128), (2, 2)))
    expert_up = normal_values(key_list[10], (EXPERTS, D, FF), D ** -0.5, 0.09375, ((0, 128), (2, 2)))
    expert_down = normal_values(key_list[11], (EXPERTS, FF, D), FF ** -0.5, 0.21875, ((0, 128), (1, 2)))
    expert_ids_keys = jax.random.split(jax.random.fold_in(key_list[12], 1), ROWS // TOK_DEV)
    expert_ids_turns = jax.random.permutation(jax.random.fold_in(key_list[12], 3), ROWS // TOK_DEV)
    expert_ids = jax.vmap(lambda own, number: shared_out(jax.random.fold_in(key_list[12], 2), own, number, TOK_DEV, EXPERTS, TOPK, CAP, 2))(expert_ids_keys, expert_ids_turns).reshape((ROWS, TOPK))
    gate_levels = with_ends(jax.random.randint(key_list[13], (ROWS, TOPK), 1, 256), jax.random.fold_in(key_list[13], 1), 1, 255).astype(jnp.int32)
    return dict(hidden=hidden, queries=queries, cache_keys=cache_keys, cache_values=cache_values, new_keys=new_keys, new_values=new_values, lengths=lengths, out_proj=out_proj, norm_gain=norm_gain, expert_gate=expert_gate, expert_up=expert_up, expert_down=expert_down, expert_ids=expert_ids, gate_levels=gate_levels)


def attend_block(query_rows, key_rows, value_rows, key_new, value_new, valid_len):
    row_count = query_rows.shape[0]
    kv_heads = key_rows.shape[2]
    group_size = query_rows.shape[1] // kv_heads
    head_dim = query_rows.shape[2]
    scaling = 1.0 / math.sqrt(head_dim)
    query_f = query_rows.astype(jnp.float32).reshape(row_count, kv_heads, group_size, head_dim)
    scores = jnp.einsum('bhgd,bthd->bhgt', query_f, key_rows.astype(jnp.float32)) * scaling
    scores_new = jnp.einsum('bhgd,bhd->bhg', query_f, key_new.astype(jnp.float32)) * scaling
    positions = jnp.arange(key_rows.shape[1], dtype=jnp.int32)
    usable = (positions[None, :] < valid_len[:, None])[:, None, None, :]
    masked = jnp.where(usable, scores, -1e+30)
    highest = jnp.maximum(lax.optimization_barrier(jnp.max(masked, axis=-1)), scores_new)
    exp_terms = jnp.exp(masked - highest[..., None])
    exp_new = jnp.exp(scores_new - highest)
    totals = lax.optimization_barrier(jnp.sum(exp_terms, axis=-1)) + exp_new
    weights = (exp_terms / totals[..., None]).astype(jnp.bfloat16)
    weight_new = (exp_new / totals).astype(jnp.bfloat16)
    blended = jnp.einsum('bhgt,bthd->bhgd', weights.astype(jnp.float32), value_rows.astype(jnp.float32))
    blended = blended + weight_new.astype(jnp.float32)[..., None] * value_new.astype(jnp.float32)[:, :, None, :]
    return blended.astype(jnp.bfloat16).reshape(row_count, kv_heads * group_size * head_dim)

def expert_halves(rows_in, gate_w, up_w, down_w):
    half_width = gate_w.shape[1] // 2
    pieces = []
    for half_index in range(2):
        low_edge = half_index * half_width
        gate_part = jnp.dot(rows_in, gate_w[:, low_edge:low_edge + half_width], preferred_element_type=jnp.float32)
        up_part = jnp.dot(rows_in, up_w[:, low_edge:low_edge + half_width], preferred_element_type=jnp.float32)
        active = (jax.nn.silu(gate_part) * up_part).astype(jnp.bfloat16)
        partial_value = jnp.dot(active, down_w[low_edge:low_edge + half_width], preferred_element_type=jnp.float32).astype(jnp.bfloat16)
        pieces.append(lax.optimization_barrier(partial_value).astype(jnp.float32))
    return (pieces[0] + pieces[1]).astype(jnp.bfloat16)

def reference(hidden, queries, cache_keys, cache_values, new_keys, new_values, lengths, out_proj, norm_gain, expert_gate, expert_up, expert_down, expert_ids, gate_levels):
    blocks = ROWS // R_DEV
    packed = (queries.reshape(blocks, R_DEV, QH, HD), cache_keys.reshape(blocks, R_DEV, CACHE, KVH, HD), cache_values.reshape(blocks, R_DEV, CACHE, KVH, HD), new_keys.reshape(blocks, R_DEV, KVH, HD), new_values.reshape(blocks, R_DEV, KVH, HD), lengths.reshape(blocks, R_DEV))
    attended = lax.map(lambda items: attend_block(*items), packed).reshape(ROWS, QH * HD)
    residual = hidden.astype(jnp.float32) + jnp.dot(attended, out_proj, preferred_element_type=jnp.float32)
    normed = (residual * lax.rsqrt(lax.optimization_barrier(jnp.mean(residual * residual, axis=-1, keepdims=True)) + 1e-06) * norm_gain).astype(jnp.bfloat16)
    flat_ids = expert_ids.reshape(-1).astype(jnp.int32)
    entries = flat_ids.shape[0]
    one_hot = (flat_ids[:, None] == jnp.arange(EXPERTS, dtype=jnp.int32)[None, :]).astype(jnp.int32)
    ranks = (lax.optimization_barrier(jnp.sum(jnp.cumsum(one_hot, axis=0) * one_hot, axis=1)) - 1).astype(jnp.int32)
    slot_total = 2 * EXPERTS * CAP
    source_row = (jnp.arange(entries, dtype=jnp.int32) // TOPK).astype(jnp.int32)
    levels = gate_levels.astype(jnp.float32)
    shares = (levels / lax.optimization_barrier(jnp.sum(levels, axis=1, keepdims=True))).reshape(-1)
    table = jnp.full((EXPERTS, slot_total), ROWS, jnp.int32).at[flat_ids, ranks].set(source_row)
    share_table = jnp.zeros((EXPERTS, slot_total), jnp.float32).at[flat_ids, ranks].set(shares)
    padded = jnp.concatenate([normed, jnp.zeros((1, D), jnp.bfloat16)], axis=0)

    def run_expert(carry, packed_expert):
        rows_index, share_row, gate_w, up_w, down_w = packed_expert
        produced = expert_halves(padded[rows_index], gate_w, up_w, down_w)
        carry = carry.at[rows_index].add(share_row[:, None] * produced.astype(jnp.float32))
        return (carry, None)
    start_sum = jnp.zeros((ROWS + 1, D), jnp.float32)
    mixture, _ = lax.scan(run_expert, start_sum, (table, share_table, expert_gate, expert_up, expert_down))
    return (residual + mixture[:ROWS]).astype(jnp.bfloat16)
```

```python
import math

import jax
import jax.numpy as jnp
from jax import lax
from jax.sharding import Mesh
from jax.sharding import PartitionSpec as P

AXES = ("role", "xh", "y", "zq", "zp", "head")
DEV = ("xh", "y", "zq", "zp")
EXPERT = ("role",) + DEV
ROWS_FROM = ("role", "xh", "y")
SUMS_TO = ("role", "xh", "y", "head")
NEAR = ("zq", "head")
FAR = ("role", "xh", "y", "zp")
CAP = 2


def attend_block(query_rows, key_rows, value_rows, key_new, value_new, valid_len):
    row_count = query_rows.shape[0]
    kv_heads = key_rows.shape[2]
    group_size = query_rows.shape[1] // kv_heads
    head_dim = query_rows.shape[2]
    scaling = 1.0 / math.sqrt(head_dim)
    query_f = query_rows.astype(jnp.float32).reshape(row_count, kv_heads, group_size, head_dim)
    scores = jnp.einsum("bhgd,bthd->bhgt", query_f, key_rows.astype(jnp.float32)) * scaling
    scores_new = jnp.einsum("bhgd,bhd->bhg", query_f, key_new.astype(jnp.float32)) * scaling
    positions = jnp.arange(key_rows.shape[1], dtype=jnp.int32)
    usable = (positions[None, :] < valid_len[:, None])[:, None, None, :]
    masked = jnp.where(usable, scores, -1e30)
    highest = jnp.maximum(jnp.max(masked, axis=-1), scores_new)
    exp_terms = jnp.exp(masked - highest[..., None])
    exp_new = jnp.exp(scores_new - highest)
    totals = jnp.sum(exp_terms, axis=-1) + exp_new
    weights = (exp_terms / totals[..., None]).astype(jnp.bfloat16)
    weight_new = (exp_new / totals).astype(jnp.bfloat16)
    blended = jnp.einsum("bhgt,bthd->bhgd", weights, value_rows, preferred_element_type=jnp.float32)
    blended = (
        blended
        + weight_new.astype(jnp.float32)[..., None] * value_new.astype(jnp.float32)[:, :, None, :]
    )
    return blended.astype(jnp.bfloat16).reshape(row_count, kv_heads * group_size * head_dim)


def swap(blocks, axes):
    return lax.all_to_all(blocks, axes, split_axis=0, concat_axis=0, tiled=True)


def project(attended, out_proj):
    rows, features = attended.shape
    half = features // 2
    role = lax.axis_index("role")
    own_weights = lax.dynamic_slice_in_dim(out_proj.T, role * half, half, axis=1)
    weights = lax.all_gather(own_weights, ("zq", "zp"), axis=0, tiled=True)
    near = lax.axis_size("xh") * lax.axis_size("y")
    halves = attended.reshape(rows, 2, half).transpose(1, 0, 2)
    sent = jnp.broadcast_to(halves[:, None], (2, near, rows, half)).reshape(2 * near, rows, half)
    gathered = swap(sent, ROWS_FROM).reshape(2 * near * rows, half)
    columns = lax.dot_general(
        gathered, weights, (((1,), (1,)), ((), ())), preferred_element_type=jnp.float32
    ).astype(jnp.bfloat16)
    tokens = rows // 2
    width = columns.shape[1]
    arrived = swap(columns.reshape(4 * near, tokens, width), SUMS_TO)
    summed = jnp.sum(arrived.reshape(2, near, 2, tokens, width).astype(jnp.float32), axis=(0, 2))
    return summed.transpose(1, 0, 2).reshape(tokens, near * width)


def slot_tables(ids, levels):
    blocks, tokens, top_k = ids.shape
    far = [lax.axis_size(name) for name in FAR]
    place = jnp.arange(math.prod(far), dtype=jnp.int32)
    pair = place % far[3]
    y_at = place // far[3] % far[2]
    x_at = place // (far[3] * far[2]) % far[1]
    role_at = place // (far[3] * far[2] * far[1])
    quad = lax.axis_size("zq")
    expert = (
        ((role_at * far[1] + x_at) * far[2] + y_at) * quad + lax.axis_index("zq")
    ) * far[3] + pair
    values = levels.astype(jnp.float32)
    shares = values / jnp.sum(values, axis=-1, keepdims=True)
    hits = (ids[None] == expert[:, None, None, None]).astype(jnp.float32)
    named = jnp.sum(hits, axis=-1)
    share = jnp.sum(hits * shares[None], axis=-1)
    earlier = jnp.cumsum(named, axis=2) - named
    slot = jnp.arange(CAP, dtype=jnp.float32)
    chosen = (earlier[:, :, None] == slot[:, None]) & (named[:, :, None] > 0)
    same = jnp.arange(blocks)[:, None] == jnp.arange(blocks)[None]
    picks = (chosen[:, :, :, None] & same[:, None, :, None]).reshape(
        len(place) * blocks * CAP, blocks * tokens
    )
    scaled = jnp.where(
        chosen[:, :, :, None] & same[:, None, :, None], share[:, :, None, None], 0.0
    ).reshape(len(place) * blocks * CAP, blocks * tokens)
    return picks.astype(jnp.bfloat16), scaled


def on_device(
    hidden,
    queries,
    cache_keys,
    cache_values,
    new_keys,
    new_values,
    lengths,
    out_proj,
    norm_gain,
    expert_gate,
    expert_up,
    expert_down,
    expert_ids,
    gate_levels,
):
    tokens, width = hidden.shape
    near = lax.axis_size("zq") * lax.axis_size("head")
    far = math.prod(lax.axis_size(name) for name in FAR)
    choices = lax.all_gather(jnp.stack([expert_ids, gate_levels]), NEAR, axis=0)
    picks, scaled = slot_tables(choices[:, 0], choices[:, 1])
    high = scaled.astype(jnp.bfloat16)
    low = (scaled - high.astype(jnp.float32)).astype(jnp.bfloat16)

    attended = attend_block(queries, cache_keys, cache_values, new_keys, new_values, lengths)
    residual = hidden.astype(jnp.float32) + project(attended, out_proj)
    normed = (
        residual
        * lax.rsqrt(jnp.mean(residual * residual, axis=-1, keepdims=True) + 1e-06)
        * norm_gain
    ).astype(jnp.bfloat16)

    pool = swap(jnp.broadcast_to(normed[None], (near, tokens, width)), NEAR)
    outgoing = jnp.dot(
        picks, pool.reshape(near * tokens, width), preferred_element_type=jnp.float32
    ).astype(jnp.bfloat16)
    slots = near * CAP
    incoming = swap(outgoing.reshape(far, slots, width), FAR).reshape(far * slots, width)
    gate_part = jnp.dot(incoming, expert_gate[0], preferred_element_type=jnp.float32)
    up_part = jnp.dot(incoming, expert_up[0], preferred_element_type=jnp.float32)
    active = (jax.nn.silu(gate_part) * up_part).astype(jnp.bfloat16)
    half_out = jnp.dot(active, expert_down[0], preferred_element_type=jnp.float32).astype(
        jnp.bfloat16
    )
    returned = swap(half_out.reshape(far, slots, width), FAR).reshape(far * slots, width)
    over_slots = (((0,), (0,)), ((), ()))
    mixed = lax.dot_general(high, returned, over_slots, preferred_element_type=jnp.float32)
    mixed = mixed + lax.dot_general(low, returned, over_slots, preferred_element_type=jnp.float32)
    parts = swap(mixed.astype(jnp.bfloat16).reshape(near, tokens, width), NEAR)
    mixture = jnp.sum(parts.astype(jnp.float32), axis=0)
    return (residual + mixture).astype(jnp.bfloat16)


def solution(mesh):
    fine = Mesh(mesh.devices.reshape(2, 2, 4, 4, 2, 2), AXES)
    token = EXPERT + ("head",)
    placed = (
        P(token, None),
        P(EXPERT, "head", None),
        P(EXPERT, None, "head", None),
        P(EXPERT, None, "head", None),
        P(EXPERT, "head", None),
        P(EXPERT, "head", None),
        P(EXPERT),
        P("head", DEV),
        P(),
        P(EXPERT, None, "head"),
        P(EXPERT, None, "head"),
        P(EXPERT, "head", None),
        P(token, None),
        P(token, None),
    )
    return jax.shard_map(
        on_device,
        mesh=fine,
        in_specs=placed,
        out_specs=P(token, None),
        check_vma=False,
    )
```

```python
import math

import jax
import jax.numpy as jnp
from jax import lax
from jax.experimental import pallas as pl
from jax.experimental.pallas import tpu as pltpu
from jax.sharding import Mesh
from jax.sharding import PartitionSpec as P

AXES = ("role", "xh", "y", "zq", "zp", "head")
DEV = ("xh", "y", "zq", "zp")
EXPERT = ("role",) + DEV
ROWS_FROM = ("role", "xh", "zq")
SUMS_TO = ("role", "xh", "zq", "head")
NEAR = ("zq", "head")
FAR = ("role", "xh", "y", "zp")
CAP = 2
BLOCK = 8
SLOTS = 16
LANES = 128


def attend_block(query_rows, key_rows, value_rows, key_new, value_new, valid_len):
    row_count = query_rows.shape[0]
    kv_heads = key_rows.shape[2]
    group_size = query_rows.shape[1] // kv_heads
    head_dim = query_rows.shape[2]
    scaling = 1.0 / math.sqrt(head_dim)
    query_f = query_rows.astype(jnp.float32).reshape(row_count, kv_heads, group_size, head_dim)
    scores = jnp.einsum("bhgd,bthd->bhgt", query_f, key_rows.astype(jnp.float32)) * scaling
    scores_new = jnp.einsum("bhgd,bhd->bhg", query_f, key_new.astype(jnp.float32)) * scaling
    positions = jnp.arange(key_rows.shape[1], dtype=jnp.int32)
    usable = (positions[None, :] < valid_len[:, None])[:, None, None, :]
    masked = jnp.where(usable, scores, -1e30)
    highest = jnp.maximum(jnp.max(masked, axis=-1), scores_new)
    exp_terms = jnp.exp(masked - highest[..., None])
    exp_new = jnp.exp(scores_new - highest)
    totals = jnp.sum(exp_terms, axis=-1) + exp_new
    weights = (exp_terms / totals[..., None]).astype(jnp.bfloat16)
    weight_new = (exp_new / totals).astype(jnp.bfloat16)
    blended = jnp.einsum("bhgt,bthd->bhgd", weights, value_rows, preferred_element_type=jnp.float32)
    blended = (
        blended
        + weight_new.astype(jnp.float32)[..., None] * value_new.astype(jnp.float32)[:, :, None, :]
    )
    return blended.astype(jnp.bfloat16).reshape(row_count, kv_heads * group_size * head_dim)


def swap(blocks, axes):
    return lax.all_to_all(blocks, axes, split_axis=0, concat_axis=0, tiled=True)


def shift(block, axis, by):
    count = lax.axis_size(axis)
    return lax.ppermute(block, axis, [(at, (at + by) % count) for at in range(count)])


def call(kernel, out_shape, *operands, spaces=None):
    whole = pl.BlockSpec(memory_space=pltpu.VMEM)
    return pl.pallas_call(
        kernel,
        out_shape=out_shape,
        in_specs=[
            pl.BlockSpec(memory_space=pltpu.SMEM) if operand.dtype == jnp.int32 else whole
            for operand in operands
        ],
        out_specs=jax.tree.map(lambda _: whole, out_shape),
    )(*operands)


def project_kernel(at_ref, rows_ref, *refs):
    pieces, out_ref = refs[:-1], refs[-1]
    count = len(pieces)
    rows = rows_ref[...]
    for by, piece_ref in enumerate(pieces):
        width = piece_ref.shape[0]
        place = lax.rem(at_ref[0] - by + count, count)
        part = lax.dot_general(
            rows, piece_ref[...], (((1,), (1,)), ((), ())), preferred_element_type=jnp.float32
        )
        out_ref[:, pl.ds(pl.multiple_of(place * width, width), width)] = part.astype(jnp.bfloat16)


def norm_kernel(arrived_ref, hidden_ref, gain_ref, choices_ref, residual_ref, sent_ref):
    roles, halves, quads, heads, tokens, width = arrived_ref.shape
    rows = width // LANES
    total = jnp.zeros((tokens, LANES), jnp.float32)
    for x in range(halves):
        for q in range(quads):
            for y in range(rows):
                span = slice(y * LANES, (y + 1) * LANES)
                first = ((x * rows + y) * quads + q) * LANES
                to = slice(first, first + LANES)
                value = hidden_ref[:, to].astype(jnp.float32)
                for r in range(roles):
                    for h in range(heads):
                        value = value + arrived_ref[r, x, q, h, :, span].astype(jnp.float32)
                residual_ref[:, to] = value
                total = total + value * value
    count = residual_ref.shape[1]
    scale = lax.rsqrt(jnp.sum(total, axis=1, keepdims=True) / count + 1e-06)
    normed = (residual_ref[...] * scale * gain_ref[...]).astype(jnp.bfloat16)
    for copy in range(sent_ref.shape[0]):
        sent_ref[copy, :, :count] = normed
        sent_ref[copy, :, count:] = choices_ref[...]


def pick_kernel(top_k, quad_ref, choices_ref, pool_ref, out_ref, scaled_ref, picks):
    count, tokens = picks.shape

    @pl.when(pl.program_id(0) == 0)
    def _():
        table = choices_ref[...].astype(jnp.float32).T
        slot = lax.broadcasted_iota(jnp.int32, (count, tokens), 0)
        token = lax.broadcasted_iota(jnp.int32, (count, tokens), 1)
        place = slot // SLOTS
        expert = place // 2 * 8 + quad_ref[0] * 2 + place % 2
        expert = expert.astype(jnp.float32)
        levels = table[top_k : 2 * top_k]
        shares = levels / jnp.sum(levels, axis=0, keepdims=True)
        named = jnp.zeros((count, tokens), jnp.float32)
        share = jnp.zeros((count, tokens), jnp.float32)
        for at in range(top_k):
            hit = table[at : at + 1] == expert
            named = named + jnp.where(hit, 1.0, 0.0)
            share = share + jnp.where(hit, shares[at : at + 1], 0.0)
        row = lax.broadcasted_iota(jnp.int32, (tokens, tokens), 0)
        col = lax.broadcasted_iota(jnp.int32, (tokens, tokens), 1)
        before = jnp.where((row // BLOCK == col // BLOCK) & (row < col), 1.0, 0.0)
        earlier = jnp.dot(
            named.astype(jnp.bfloat16),
            before.astype(jnp.bfloat16),
            preferred_element_type=jnp.float32,
        )
        rank = (slot % CAP).astype(jnp.float32)
        chosen = (named > 0) & (earlier == rank) & (token // BLOCK == slot % SLOTS // CAP)
        picks[...] = jnp.where(chosen, 1.0, 0.0).astype(jnp.bfloat16)
        scaled_ref[...] = jnp.where(chosen, share, 0.0).astype(jnp.bfloat16)

    out_ref[...] = jnp.dot(
        picks[...], pool_ref[...], preferred_element_type=jnp.float32
    ).astype(jnp.bfloat16)


def pick_rows(pool, width, top_k):
    tokens = pool.shape[0]
    count = math.prod(lax.axis_size(name) for name in FAR) * SLOTS
    block = 1024
    quad = lax.axis_index("zq").astype(jnp.int32).reshape(1)
    return pl.pallas_call(
        lambda *refs: pick_kernel(top_k, *refs),
        out_shape=(
            jax.ShapeDtypeStruct((count, width), jnp.bfloat16),
            jax.ShapeDtypeStruct((count, tokens), jnp.bfloat16),
        ),
        grid=(width // block,),
        in_specs=[
            pl.BlockSpec(memory_space=pltpu.SMEM),
            pl.BlockSpec((tokens, LANES), lambda s: (0, width // LANES)),
            pl.BlockSpec((tokens, block), lambda s: (0, s)),
        ],
        out_specs=(
            pl.BlockSpec((count, block), lambda s: (0, s)),
            pl.BlockSpec((count, tokens), lambda s: (0, 0)),
        ),
        scratch_shapes=[pltpu.VMEM((count, tokens), jnp.bfloat16)],
        compiler_params=pltpu.CompilerParams(
            dimension_semantics=("arbitrary",), vmem_limit_bytes=16 << 20
        ),
    )(quad, pool, pool)


def ffn_kernel(unit_steps, rows_ref, gate_ref, up_ref, down_ref, out_ref, active):
    step = pl.program_id(0)

    @pl.when(step < unit_steps)
    def _():
        units = gate_ref.shape[1]
        both = jnp.dot(
            rows_ref[...],
            jnp.concatenate([gate_ref[...], up_ref[...]], axis=1),
            preferred_element_type=jnp.float32,
        )
        gated = jax.nn.silu(both[:, :units]) * both[:, units:]
        to = pl.ds(pl.multiple_of(step * units, units), units)
        active[:, to] = gated.astype(jnp.bfloat16)

    @pl.when(step >= unit_steps)
    def _():
        out_ref[...] = jnp.dot(
            active[...], down_ref[...], preferred_element_type=jnp.float32
        ).astype(jnp.bfloat16)


def expert_rows(rows, gate, up, down):
    count, width = rows.shape
    units = gate.shape[2]
    block, columns = LANES, 1024
    steps = units // block

    def early(step):
        return jnp.minimum(step, steps - 1)

    def late(step):
        return jnp.maximum(step - steps, 0)

    return pl.pallas_call(
        lambda *refs: ffn_kernel(steps, *refs),
        out_shape=jax.ShapeDtypeStruct((count, width), jnp.bfloat16),
        grid=(steps + width // columns,),
        in_specs=[
            pl.BlockSpec((count, width), lambda s: (0, 0), pipeline_mode=pl.Buffered(1)),
            pl.BlockSpec((None, width, block), lambda s: (0, 0, early(s))),
            pl.BlockSpec((None, width, block), lambda s: (0, 0, early(s))),
            pl.BlockSpec((None, units, columns), lambda s: (0, 0, late(s))),
        ],
        out_specs=pl.BlockSpec((count, columns), lambda s: (0, late(s))),
        scratch_shapes=[pltpu.VMEM((count, units), jnp.bfloat16)],
        compiler_params=pltpu.CompilerParams(
            dimension_semantics=("arbitrary",), vmem_limit_bytes=24 << 20
        ),
        cost_estimate=pl.CostEstimate(
            flops=6 * count * width * units,
            bytes_accessed=2 * (2 * count * width + 3 * width * units),
            transcendentals=count * units,
        ),
    )(rows, gate, up, down)


def weight_pair(out_proj):
    cols = out_proj.shape[1]
    half = out_proj.shape[0] // 2
    own = lax.dynamic_slice_in_dim(out_proj.T, lax.axis_index("role") * half, half, axis=1)
    other = shift(own, "zp", 1)
    first = lax.axis_index("zp") == 0
    pair = jnp.where(
        first, jnp.concatenate([own, other], axis=0), jnp.concatenate([other, own], axis=0)
    )
    return pair


def project(attended, pair):
    rows, features = attended.shape
    half = features // 2
    near = lax.axis_size("xh") * lax.axis_size("zq")
    halves = attended.reshape(rows, 2, half).transpose(1, 0, 2)
    sent = jnp.broadcast_to(halves[:, None], (2, near, rows, half)).reshape(2 * near, rows, half)
    sent, pair = lax.optimization_barrier((sent, pair))
    pieces = [pair] + [shift(pair, "y", by) for by in range(1, lax.axis_size("y"))]
    gathered = swap(sent, ROWS_FROM).reshape(2 * near * rows, half)
    width = len(pieces) * pieces[0].shape[0]
    columns = call(
        project_kernel,
        jax.ShapeDtypeStruct((2 * near * rows, width), jnp.bfloat16),
        lax.axis_index("y").astype(jnp.int32).reshape(1),
        gathered,
        *pieces,
    )
    return swap(columns.reshape(4 * near, rows // 2, width), SUMS_TO)


def on_device(
    hidden,
    queries,
    cache_keys,
    cache_values,
    new_keys,
    new_values,
    lengths,
    out_proj,
    norm_gain,
    expert_gate,
    expert_up,
    expert_down,
    expert_ids,
    gate_levels,
):
    tokens, width = hidden.shape
    top_k = expert_ids.shape[1]
    near = lax.axis_size("zq") * lax.axis_size("head")
    far = math.prod(lax.axis_size(name) for name in FAR)

    pair = weight_pair(out_proj)
    attended = attend_block(queries, cache_keys, cache_values, new_keys, new_values, lengths)
    arrived = project(attended, pair)
    choices = jnp.concatenate([expert_ids, gate_levels], axis=1).astype(jnp.bfloat16)
    choices = jnp.pad(choices, ((0, 0), (0, LANES - 2 * top_k)))
    residual, sent = call(
        norm_kernel,
        (
            jax.ShapeDtypeStruct((tokens, width), jnp.float32),
            jax.ShapeDtypeStruct((near, tokens, width + LANES), jnp.bfloat16),
        ),
        arrived.reshape([lax.axis_size(name) for name in SUMS_TO] + list(arrived.shape[1:])),
        hidden,
        norm_gain.reshape(1, width),
        choices,
    )

    pool = swap(sent, NEAR).reshape(near * tokens, width + LANES)
    outgoing, scaled = pick_rows(pool, width, top_k)
    incoming = swap(outgoing.reshape(far, SLOTS, width), FAR).reshape(far * SLOTS, width)
    half_out = expert_rows(incoming, expert_gate, expert_up, expert_down)
    returned = swap(half_out.reshape(far, SLOTS, width), FAR).reshape(far * SLOTS, width)
    mixed = lax.dot_general(
        scaled, returned, (((0,), (0,)), ((), ())), preferred_element_type=jnp.float32
    ).astype(jnp.bfloat16)
    parts = swap(mixed.reshape(near, tokens, width), NEAR)
    mixture = jnp.sum(parts.astype(jnp.float32), axis=0)
    return (residual + mixture).astype(jnp.bfloat16)


def solution(mesh):
    fine = Mesh(mesh.devices.reshape(2, 2, 4, 4, 2, 2), AXES)
    token = EXPERT + ("head",)
    placed = (
        P(token, None),
        P(EXPERT, "head", None),
        P(EXPERT, None, "head", None),
        P(EXPERT, None, "head", None),
        P(EXPERT, "head", None),
        P(EXPERT, "head", None),
        P(EXPERT),
        P("head", DEV),
        P(),
        P(EXPERT, None, "head"),
        P(EXPERT, None, "head"),
        P(EXPERT, "head", None),
        P(token, None),
        P(token, None),
    )
    return jax.shard_map(
        on_device,
        mesh=fine,
        in_specs=placed,
        out_specs=P(token, None),
        check_vma=False,
    )
```

```python
import math

import jax
import jax.numpy as jnp
from jax import lax
from jax.experimental import pallas as pl
from jax.experimental.pallas import tpu as pltpu
from jax.sharding import Mesh
from jax.sharding import PartitionSpec as P

AXES = ("role", "xh", "y", "zq", "zp", "head")
DEV = ("xh", "y", "zq", "zp")
EXPERT = ("role",) + DEV
RING = ("zq", "zp")
ROWS_FROM = ("role", "xh", "y")
SUMS_TO = ("role", "xh", "y", "head")
NEAR = "zq"
FAR = ("role", "xh", "y", "zp", "head")
CAP = 2
BLOCK = 8
SLOTS = 8
LANES = 128


def attend_block(query_rows, key_rows, value_rows, key_new, value_new, valid_len):
    row_count = query_rows.shape[0]
    kv_heads = key_rows.shape[2]
    group_size = query_rows.shape[1] // kv_heads
    head_dim = query_rows.shape[2]
    scaling = 1.0 / math.sqrt(head_dim)
    query_f = query_rows.astype(jnp.float32).reshape(row_count, kv_heads, group_size, head_dim)
    scores = jnp.einsum("bhgd,bthd->bhgt", query_f, key_rows.astype(jnp.float32)) * scaling
    scores_new = jnp.einsum("bhgd,bhd->bhg", query_f, key_new.astype(jnp.float32)) * scaling
    positions = jnp.arange(key_rows.shape[1], dtype=jnp.int32)
    usable = (positions[None, :] < valid_len[:, None])[:, None, None, :]
    masked = jnp.where(usable, scores, -1e30)
    highest = jnp.maximum(jnp.max(masked, axis=-1), scores_new)
    exp_terms = jnp.exp(masked - highest[..., None])
    exp_new = jnp.exp(scores_new - highest)
    totals = jnp.sum(exp_terms, axis=-1) + exp_new
    weights = (exp_terms / totals[..., None]).astype(jnp.bfloat16)
    weight_new = (exp_new / totals).astype(jnp.bfloat16)
    blended = jnp.einsum("bhgt,bthd->bhgd", weights, value_rows, preferred_element_type=jnp.float32)
    blended = (
        blended
        + weight_new.astype(jnp.float32)[..., None] * value_new.astype(jnp.float32)[:, :, None, :]
    )
    return blended.astype(jnp.bfloat16)


def swap(blocks, axes):
    return lax.all_to_all(blocks, axes, split_axis=0, concat_axis=0, tiled=True)


def shift(block, axis, by):
    count = lax.axis_size(axis)
    return lax.ppermute(block, axis, [(at, (at + by) % count) for at in range(count)])


def spread_kernel(attended_ref, out_ref):
    roles, near, rows, _ = out_ref.shape
    for role in range(roles):
        for head in range(attended_ref.shape[2]):
            part = attended_ref[:, role, head, :]
            for copy in range(near):
                out_ref[role, copy, :, head * LANES : (head + 1) * LANES] = part


def project_kernel(spots, at_ref, rows_ref, *refs):
    pieces, out_ref, weights = refs[:-2], refs[-2], refs[-1]
    width = pieces[0].shape[0]
    count = weights.shape[0] // width
    for (by, first), piece_ref in zip(spots, pieces):
        place = lax.rem(at_ref[0] - by + count, count) * width + first
        to = pl.ds(pl.multiple_of(place, width // 2), piece_ref.shape[0])
        weights[to, :] = piece_ref[...]
    out_ref[...] = lax.dot_general(
        rows_ref[...], weights[...], (((1,), (1,)), ((), ())), preferred_element_type=jnp.float32
    ).astype(jnp.bfloat16)


def norm_kernel(arrived_ref, hidden_ref, gain_ref, choices_ref, residual_ref, sent_ref):
    roles, halves, rings, heads, tokens, width = arrived_ref.shape
    rows = width // LANES
    total = jnp.zeros((tokens, LANES), jnp.float32)
    for x in range(halves):
        for y in range(rings):
            for z in range(rows):
                span = slice(z * LANES, (z + 1) * LANES)
                first = (x * rings + y) * width + z * LANES
                to = slice(first, first + LANES)
                value = hidden_ref[:, to].astype(jnp.float32)
                for r in range(roles):
                    for h in range(heads):
                        value = value + arrived_ref[r, x, y, h, :, span].astype(jnp.float32)
                residual_ref[:, to] = value
                total = total + value * value
    count = residual_ref.shape[1]
    scale = lax.rsqrt(jnp.sum(total, axis=1, keepdims=True) / count + 1e-06)
    sent_ref[:, :count] = (residual_ref[...] * scale * gain_ref[...]).astype(jnp.bfloat16)
    sent_ref[:, count:] = choices_ref[...]


def pick_kernel(top_k, blocks, quad_ref, *refs):
    choices_refs, pool_refs = refs[:blocks], refs[blocks : 2 * blocks]
    out_ref, scaled_ref, picks = refs[2 * blocks :]
    count, tokens = picks.shape

    @pl.when(pl.program_id(0) == 0)
    def _():
        table = jnp.concatenate([ref[...].astype(jnp.float32) for ref in choices_refs], axis=0).T
        slot = lax.broadcasted_iota(jnp.int32, (count, tokens), 0)
        token = lax.broadcasted_iota(jnp.int32, (count, tokens), 1)
        place = slot // (2 * SLOTS)
        expert = (place // 2 * 8 + quad_ref[0] * 2 + place % 2).astype(jnp.float32)
        levels = table[top_k : 2 * top_k]
        shares = levels / jnp.sum(levels, axis=0, keepdims=True)
        named = jnp.zeros((count, tokens), jnp.float32)
        share = jnp.zeros((count, tokens), jnp.float32)
        for at in range(top_k):
            hit = table[at : at + 1] == expert
            named = named + jnp.where(hit, 1.0, 0.0)
            share = share + jnp.where(hit, shares[at : at + 1], 0.0)
        row = lax.broadcasted_iota(jnp.int32, (tokens, tokens), 0)
        col = lax.broadcasted_iota(jnp.int32, (tokens, tokens), 1)
        before = jnp.where((row // BLOCK == col // BLOCK) & (row < col), 1.0, 0.0)
        earlier = jnp.dot(
            named.astype(jnp.bfloat16),
            before.astype(jnp.bfloat16),
            preferred_element_type=jnp.float32,
        )
        rank = (slot % CAP).astype(jnp.float32)
        chosen = (named > 0) & (earlier == rank) & (token // BLOCK == slot % SLOTS // CAP)
        scaled_ref[...] = jnp.where(chosen, share, 0.0).astype(jnp.bfloat16)
        picks[...] = jnp.where(chosen, 1.0, 0.0).astype(jnp.bfloat16)

    pool = jnp.concatenate([ref[...] for ref in pool_refs], axis=0)
    out_ref[...] = jnp.dot(picks[...], pool, preferred_element_type=jnp.float32).astype(
        jnp.bfloat16
    )


def pick_rows(pool, width, top_k):
    blocks, rows = len(pool), pool[0].shape[0]
    tokens = blocks * rows
    count = lax.axis_size(FAR) * SLOTS
    block = 1024
    quad = lax.axis_index("zq").astype(jnp.int32).reshape(1)
    return pl.pallas_call(
        lambda *refs: pick_kernel(top_k, blocks, *refs),
        out_shape=(
            jax.ShapeDtypeStruct((count, width), jnp.bfloat16),
            jax.ShapeDtypeStruct((count, tokens), jnp.bfloat16),
        ),
        grid=(width // block,),
        in_specs=[pl.BlockSpec(memory_space=pltpu.SMEM)]
        + [pl.BlockSpec((rows, LANES), lambda s: (0, width // LANES))] * blocks
        + [pl.BlockSpec((rows, block), lambda s: (0, s))] * blocks,
        out_specs=(
            pl.BlockSpec((count, block), lambda s: (0, s)),
            pl.BlockSpec((count, tokens), lambda s: (0, 0)),
        ),
        scratch_shapes=[pltpu.VMEM((count, tokens), jnp.bfloat16)],
        compiler_params=pltpu.CompilerParams(
            dimension_semantics=("arbitrary",), vmem_limit_bytes=16 << 20
        ),
    )(quad, *pool, *pool)


def ffn_kernel(unit_steps, rows_ref, gate_ref, up_ref, down_ref, out_ref, active):
    step = pl.program_id(0)

    @pl.when(step < unit_steps)
    def _():
        units = gate_ref.shape[1]
        both = jnp.dot(
            rows_ref[...],
            jnp.concatenate([gate_ref[...], up_ref[...]], axis=1),
            preferred_element_type=jnp.float32,
        )
        gated = jax.nn.silu(both[:, :units]) * both[:, units:]
        to = pl.ds(pl.multiple_of(step * units, units), units)
        active[:, to] = gated.astype(jnp.bfloat16)

    @pl.when(step >= unit_steps)
    def _():
        out_ref[...] = jnp.dot(
            active[...], down_ref[...], preferred_element_type=jnp.float32
        ).astype(jnp.bfloat16)


def expert_rows(rows, gate, up, down):
    count, width = rows.shape
    units = gate.shape[2]
    block, columns = LANES, 1024
    steps = units // block

    def early(step):
        return jnp.minimum(step, steps - 1)

    def late(step):
        return jnp.maximum(step - steps, 0)

    return pl.pallas_call(
        lambda *refs: ffn_kernel(steps, *refs),
        out_shape=jax.ShapeDtypeStruct((count, width), jnp.bfloat16),
        grid=(steps + width // columns,),
        in_specs=[
            pl.BlockSpec((count, width), lambda s: (0, 0), pipeline_mode=pl.Buffered(1)),
            pl.BlockSpec((None, width, block), lambda s: (0, 0, early(s))),
            pl.BlockSpec((None, width, block), lambda s: (0, 0, early(s))),
            pl.BlockSpec((None, units, columns), lambda s: (0, 0, late(s))),
        ],
        out_specs=pl.BlockSpec((count, columns), lambda s: (0, late(s))),
        scratch_shapes=[pltpu.VMEM((count, units), jnp.bfloat16)],
        compiler_params=pltpu.CompilerParams(
            dimension_semantics=("arbitrary",), vmem_limit_bytes=44 << 20
        ),
        cost_estimate=pl.CostEstimate(
            flops=6 * count * width * units,
            bytes_accessed=2 * (2 * count * width + 3 * width * units),
            transcendentals=count * units,
        ),
    )(rows, gate, up, down)


def half_weights(out_proj):
    half = out_proj.shape[0] // 2
    return lax.dynamic_slice_in_dim(out_proj.T, lax.axis_index("role") * half, half, axis=1)


def project(attended, own):
    rows, roles, group, head_dim = attended.shape
    half = group * head_dim
    near = lax.axis_size("xh") * lax.axis_size("y")
    ring, cols = lax.axis_size(RING), own.shape[0]
    up, down = shift(own, RING, 1), shift(own, RING, -1)
    attended, up, down = lax.optimization_barrier((attended, up, down))
    whole = pl.BlockSpec(memory_space=pltpu.VMEM)
    sent = pl.pallas_call(
        spread_kernel,
        out_shape=jax.ShapeDtypeStruct((roles, near, rows, half), jnp.bfloat16),
        in_specs=[whole],
        out_specs=whole,
    )(attended)
    gathered = swap(sent.reshape(roles * near, rows, half), ROWS_FROM)
    gathered = gathered.reshape(roles * near * rows, half)
    pieces, spots = [own, up, down], [(0, 0), (1, 0), (-1, 0)]
    for by in range(2, ring // 2):
        up, down = shift(up, RING, 1), shift(down, RING, -1)
        pieces, spots = pieces + [up, down], spots + [(by, 0), (-by, 0)]
    part = cols // 2
    pieces = pieces + [shift(up[:part], RING, 1), shift(down[part:], RING, -1)]
    spots = spots + [(ring // 2, 0), (ring // 2, part)]
    columns = pl.pallas_call(
        lambda *refs: project_kernel(spots, *refs),
        out_shape=jax.ShapeDtypeStruct((roles * near * rows, ring * cols), jnp.bfloat16),
        in_specs=[pl.BlockSpec(memory_space=pltpu.SMEM)] + [whole] * (len(pieces) + 1),
        out_specs=whole,
        scratch_shapes=[pltpu.VMEM((ring * cols, half), jnp.bfloat16)],
    )(lax.axis_index(RING).astype(jnp.int32).reshape(1), gathered, *pieces)
    return swap(columns.reshape(2 * roles * near, rows // 2, ring * cols), SUMS_TO)


def on_device(
    hidden,
    queries,
    cache_keys,
    cache_values,
    new_keys,
    new_values,
    lengths,
    out_proj,
    norm_gain,
    expert_gate,
    expert_up,
    expert_down,
    expert_ids,
    gate_levels,
):
    tokens, width = hidden.shape
    top_k = expert_ids.shape[1]
    near, far = lax.axis_size(NEAR), lax.axis_size(FAR)

    own = half_weights(out_proj)
    attended = attend_block(queries, cache_keys, cache_values, new_keys, new_values, lengths)
    arrived = project(attended, own)
    choices = jnp.concatenate([expert_ids, gate_levels], axis=1).astype(jnp.bfloat16)
    choices = jnp.pad(choices, ((0, 0), (0, LANES - 2 * top_k)))
    whole = pl.BlockSpec(memory_space=pltpu.VMEM)
    residual, sent = pl.pallas_call(
        norm_kernel,
        out_shape=(
            jax.ShapeDtypeStruct((tokens, width), jnp.float32),
            jax.ShapeDtypeStruct((tokens, width + LANES), jnp.bfloat16),
        ),
        in_specs=[whole] * 4,
        out_specs=(whole, whole),
    )(
        arrived.reshape([lax.axis_size(name) for name in SUMS_TO] + list(arrived.shape[1:])),
        hidden,
        norm_gain.reshape(1, width),
        choices,
    )

    pool = [sent] + [shift(sent, NEAR, by) for by in range(1, near)]
    outgoing, scaled = pick_rows(pool, width, top_k)
    incoming = swap(outgoing.reshape(far, SLOTS, width), FAR).reshape(far * SLOTS, width)
    half_out = expert_rows(incoming, expert_gate, expert_up, expert_down)
    returned = swap(half_out.reshape(far, SLOTS, width), FAR).reshape(far * SLOTS, width)
    mixed = lax.dot_general(
        scaled, returned, (((0,), (0,)), ((), ())), preferred_element_type=jnp.float32
    ).astype(jnp.bfloat16)
    parts = [mixed[:tokens]] + [
        shift(mixed[by * tokens : (by + 1) * tokens], NEAR, -by) for by in range(1, near)
    ]
    mixture = sum(part.astype(jnp.float32) for part in parts)
    return (residual + mixture).astype(jnp.bfloat16)


def solution(mesh):
    fine = Mesh(mesh.devices.reshape(2, 2, 4, 4, 2, 2), AXES)
    token = EXPERT + ("head",)
    placed = (
        P(token, None),
        P(EXPERT, "head", None),
        P(EXPERT, None, "head", None),
        P(EXPERT, None, "head", None),
        P(EXPERT, "head", None),
        P(EXPERT, "head", None),
        P(EXPERT),
        P("head", DEV),
        P(),
        P(EXPERT, None, "head"),
        P(EXPERT, None, "head"),
        P(EXPERT, "head", None),
        P(token, None),
        P(token, None),
    )
    return jax.shard_map(
        on_device,
        mesh=fine,
        in_specs=placed,
        out_specs=P(token, None),
        check_vma=False,
    )
```

```python
import math

import jax
import jax.numpy as jnp
from jax import lax
from jax.experimental import pallas as pl
from jax.experimental.pallas import tpu as pltpu
from jax.sharding import Mesh
from jax.sharding import PartitionSpec as P

AXES = ("role", "xh", "y", "zq", "zp", "head")
DEV = ("xh", "y", "zq", "zp")
EXPERT = ("role",) + DEV
RING = ("zq", "zp")
ROWS_FROM = ("role", "xh", "y")
SUMS_TO = ("role", "xh", "y", "head")
NEAR = "zq"
FAR = ("xh", "head", "y", "zp", "role")
CAP = 2
BLOCK = 8
SLOTS = 8
LANES = 128


def attend_block(query_rows, key_rows, value_rows, key_new, value_new, valid_len):
    row_count = query_rows.shape[0]
    kv_heads = key_rows.shape[2]
    group_size = query_rows.shape[1] // kv_heads
    head_dim = query_rows.shape[2]
    scaling = 1.0 / math.sqrt(head_dim)
    query_f = query_rows.astype(jnp.float32).reshape(row_count, kv_heads, group_size, head_dim)
    scores = jnp.einsum("bhgd,bthd->bhgt", query_f, key_rows.astype(jnp.float32)) * scaling
    scores_new = jnp.einsum("bhgd,bhd->bhg", query_f, key_new.astype(jnp.float32)) * scaling
    positions = jnp.arange(key_rows.shape[1], dtype=jnp.int32)
    usable = (positions[None, :] < valid_len[:, None])[:, None, None, :]
    masked = jnp.where(usable, scores, -1e30)
    highest = jnp.maximum(jnp.max(masked, axis=-1), scores_new)
    exp_terms = jnp.exp(masked - highest[..., None])
    exp_new = jnp.exp(scores_new - highest)
    totals = jnp.sum(exp_terms, axis=-1) + exp_new
    weights = (exp_terms / totals[..., None]).astype(jnp.bfloat16)
    weight_new = (exp_new / totals).astype(jnp.bfloat16)
    blended = jnp.einsum("bhgt,bthd->bhgd", weights, value_rows, preferred_element_type=jnp.float32)
    blended = (
        blended
        + weight_new.astype(jnp.float32)[..., None] * value_new.astype(jnp.float32)[:, :, None, :]
    )
    return blended.astype(jnp.bfloat16)


def swap(blocks, axes):
    return lax.all_to_all(blocks, axes, split_axis=0, concat_axis=0, tiled=True)


def shift(block, axis, by):
    count = lax.axis_size(axis)
    return lax.ppermute(block, axis, [(at, (at + by) % count) for at in range(count)])


def held(memory, *arrays):
    return [pltpu.with_memory_space_constraint(array, memory) for array in arrays]


def spread_kernel(attended_ref, out_ref):
    roles, near, rows, _ = out_ref.shape
    for role in range(roles):
        for head in range(attended_ref.shape[2]):
            part = attended_ref[:, role, head, :]
            for copy in range(near):
                out_ref[role, copy, :, head * LANES : (head + 1) * LANES] = part


def project_kernel(spots, at_ref, rows_ref, *refs):
    pieces, out_ref, weights = refs[:-2], refs[-2], refs[-1]
    width = pieces[0].shape[0]
    count = weights.shape[0] // width
    for (by, first), piece_ref in zip(spots, pieces):
        place = lax.rem(at_ref[0] - by + count, count) * width + first
        to = pl.ds(pl.multiple_of(place, width // 2), piece_ref.shape[0])
        weights[to, :] = piece_ref[...]
    out_ref[...] = lax.dot_general(
        rows_ref[...], weights[...], (((1,), (1,)), ((), ())), preferred_element_type=jnp.float32
    ).astype(jnp.bfloat16)


def norm_kernel(arrived_ref, hidden_ref, gain_ref, choices_ref, residual_ref, sent_ref):
    roles, halves, rings, heads, tokens, width = arrived_ref.shape
    rows = width // LANES
    total = jnp.zeros((tokens, LANES), jnp.float32)
    for x in range(halves):
        for y in range(rings):
            for z in range(rows):
                span = slice(z * LANES, (z + 1) * LANES)
                first = (x * rings + y) * width + z * LANES
                to = slice(first, first + LANES)
                value = hidden_ref[:, to].astype(jnp.float32)
                for r in range(roles):
                    for h in range(heads):
                        value = value + arrived_ref[r, x, y, h, :, span].astype(jnp.float32)
                residual_ref[:, to] = value
                total = total + value * value
    count = residual_ref.shape[1]
    scale = lax.rsqrt(jnp.sum(total, axis=1, keepdims=True) / count + 1e-06)
    sent_ref[:, :count] = (residual_ref[...] * scale * gain_ref[...]).astype(jnp.bfloat16)
    sent_ref[:, count:] = choices_ref[...]


def pick_kernel(top_k, blocks, quad_ref, *refs):
    choices_refs, pool_refs = refs[:blocks], refs[blocks : 2 * blocks]
    out_ref, scaled_ref, picks = refs[2 * blocks :]
    count, tokens = picks.shape

    @pl.when(pl.program_id(0) == 0)
    def _():
        table = jnp.concatenate([ref[...].astype(jnp.float32) for ref in choices_refs], axis=0).T
        slot = lax.broadcasted_iota(jnp.int32, (count, tokens), 0)
        token = lax.broadcasted_iota(jnp.int32, (count, tokens), 1)
        far = slot // SLOTS
        chip = far // 32 * 4 + far // 4 % 4
        expert = far % 2 * 64 + chip * 8 + quad_ref[0] * 2 + far // 2 % 2
        expert = expert.astype(jnp.float32)
        levels = table[top_k : 2 * top_k]
        shares = levels / jnp.sum(levels, axis=0, keepdims=True)
        named = jnp.zeros((count, tokens), jnp.float32)
        share = jnp.zeros((count, tokens), jnp.float32)
        for at in range(top_k):
            hit = table[at : at + 1] == expert
            named = named + jnp.where(hit, 1.0, 0.0)
            share = share + jnp.where(hit, shares[at : at + 1], 0.0)
        row = lax.broadcasted_iota(jnp.int32, (tokens, tokens), 0)
        col = lax.broadcasted_iota(jnp.int32, (tokens, tokens), 1)
        before = jnp.where((row // BLOCK == col // BLOCK) & (row < col), 1.0, 0.0)
        earlier = jnp.dot(
            named.astype(jnp.bfloat16),
            before.astype(jnp.bfloat16),
            preferred_element_type=jnp.float32,
        )
        rank = (slot % CAP).astype(jnp.float32)
        chosen = (named > 0) & (earlier == rank) & (token // BLOCK == slot % SLOTS // CAP)
        scaled_ref[...] = jnp.where(chosen, share, 0.0).astype(jnp.bfloat16)
        picks[...] = jnp.where(chosen, 1.0, 0.0).astype(jnp.bfloat16)

    pool = jnp.concatenate([ref[...] for ref in pool_refs], axis=0)
    out_ref[...] = jnp.dot(picks[...], pool, preferred_element_type=jnp.float32).astype(
        jnp.bfloat16
    )


def pick_rows(pool, width, top_k):
    blocks, rows = len(pool), pool[0].shape[0]
    tokens = blocks * rows
    count = lax.axis_size(FAR) * SLOTS
    block = 1024
    quad = lax.axis_index("zq").astype(jnp.int32).reshape(1)
    return pl.pallas_call(
        lambda *refs: pick_kernel(top_k, blocks, *refs),
        out_shape=(
            jax.ShapeDtypeStruct((count, width), jnp.bfloat16),
            jax.ShapeDtypeStruct((count, tokens), jnp.bfloat16),
        ),
        grid=(width // block,),
        in_specs=[pl.BlockSpec(memory_space=pltpu.SMEM)]
        + [pl.BlockSpec((rows, LANES), lambda s: (0, width // LANES))] * blocks
        + [pl.BlockSpec((rows, block), lambda s: (0, s))] * blocks,
        out_specs=(
            pl.BlockSpec((count, block), lambda s: (0, s)),
            pl.BlockSpec((count, tokens), lambda s: (0, 0)),
        ),
        scratch_shapes=[pltpu.VMEM((count, tokens), jnp.bfloat16)],
        compiler_params=pltpu.CompilerParams(
            dimension_semantics=("arbitrary",), vmem_limit_bytes=16 << 20
        ),
    )(quad, *held(pltpu.HBM, pool[0]), *pool[1:], *held(pltpu.HBM, pool[0]), *pool[1:])


def ffn_kernel(unit_steps, rows_ref, gate_ref, up_ref, down_hbm, out_ref, active, down_ref, arrival):
    step = pl.program_id(0)
    fetch = pltpu.make_async_copy(down_hbm, down_ref, arrival)

    @pl.when(step == 0)
    def _():
        fetch.start()

    @pl.when(step == unit_steps)
    def _():
        fetch.wait()

    @pl.when(step < unit_steps)
    def _():
        to = pl.ds(pl.multiple_of(step * LANES, LANES), LANES)
        both = jnp.dot(
            rows_ref[...],
            jnp.concatenate([gate_ref[0, :, to], up_ref[0, :, to]], axis=1),
            preferred_element_type=jnp.float32,
        )
        gated = jax.nn.silu(both[:, :LANES]) * both[:, LANES:]
        active[:, to] = gated.astype(jnp.bfloat16)

    @pl.when(step >= unit_steps)
    def _():
        columns = out_ref.shape[1]
        first = jnp.maximum(step - unit_steps, 0) * columns
        out_ref[...] = jnp.dot(
            active[...],
            down_ref[0, :, pl.ds(pl.multiple_of(first, columns), columns)],
            preferred_element_type=jnp.float32,
        ).astype(jnp.bfloat16)


def expert_rows(rows, gate, up, down):
    count, width = rows.shape
    units = gate.shape[2]
    columns = 1024
    steps = units // LANES
    whole = pl.BlockSpec(memory_space=pltpu.VMEM)
    return pl.pallas_call(
        lambda *refs: ffn_kernel(steps, *refs),
        out_shape=jax.ShapeDtypeStruct((count, width), jnp.bfloat16),
        grid=(steps + width // columns,),
        in_specs=[whole] * 3 + [pl.BlockSpec(memory_space=pl.ANY)],
        out_specs=pl.BlockSpec((count, columns), lambda s: (0, jnp.maximum(s - steps, 0))),
        scratch_shapes=[
            pltpu.VMEM((count, units), jnp.bfloat16),
            pltpu.VMEM(down.shape, jnp.bfloat16),
            pltpu.SemaphoreType.DMA,
        ],
        compiler_params=pltpu.CompilerParams(
            dimension_semantics=("arbitrary",), vmem_limit_bytes=16 << 20
        ),
        cost_estimate=pl.CostEstimate(
            flops=6 * count * width * units,
            bytes_accessed=2 * (2 * count * width + 3 * width * units),
            transcendentals=count * units,
        ),
    )(*held(pltpu.VMEM, rows, gate, up), *held(pltpu.HBM, down))


def half_weights(out_proj):
    half = out_proj.shape[0] // 2
    return lax.dynamic_slice_in_dim(out_proj.T, lax.axis_index("role") * half, half, axis=1)


def project(attended, own):
    rows, roles, group, head_dim = attended.shape
    half = group * head_dim
    near = lax.axis_size("xh") * lax.axis_size("y")
    ring, cols = lax.axis_size(RING), own.shape[0]
    up, down = shift(own, RING, 1), shift(own, RING, -1)
    whole = pl.BlockSpec(memory_space=pltpu.VMEM)
    sent = pl.pallas_call(
        spread_kernel,
        out_shape=jax.ShapeDtypeStruct((roles, near, rows, half), jnp.bfloat16),
        in_specs=[whole],
        out_specs=whole,
    )(attended)
    sent, up, down = lax.optimization_barrier((sent, up, down))
    pieces, spots = [own, up, down], [(0, 0), (1, 0), (-1, 0)]
    gathered = swap(sent.reshape(roles * near, rows, half), ROWS_FROM)
    gathered = gathered.reshape(roles * near * rows, half)
    for by in range(2, ring // 2):
        up, down = shift(up, RING, 1), shift(down, RING, -1)
        pieces, spots = pieces + [up, down], spots + [(by, 0), (-by, 0)]
    part = cols // 2
    pieces = pieces + [shift(up[:part], RING, 1), shift(down[part:], RING, -1)]
    spots = spots + [(ring // 2, 0), (ring // 2, part)]
    columns = pl.pallas_call(
        lambda *refs: project_kernel(spots, *refs),
        out_shape=jax.ShapeDtypeStruct((roles * near * rows, ring * cols), jnp.bfloat16),
        grid=(1,),
        in_specs=[pl.BlockSpec(memory_space=pltpu.SMEM)] + [whole] * (len(pieces) + 1),
        out_specs=pl.BlockSpec((roles * near * rows, ring * cols), lambda s: (0, 0)),
        scratch_shapes=[pltpu.VMEM((ring * cols, half), jnp.bfloat16)],
    )(lax.axis_index(RING).astype(jnp.int32).reshape(1), *held(pltpu.VMEM, gathered, *pieces))
    return swap(columns.reshape(2 * roles * near, rows // 2, ring * cols), SUMS_TO)


def on_device(
    hidden,
    queries,
    cache_keys,
    cache_values,
    new_keys,
    new_values,
    lengths,
    out_proj,
    norm_gain,
    expert_gate,
    expert_up,
    expert_down,
    expert_ids,
    gate_levels,
):
    tokens, width = hidden.shape
    top_k = expert_ids.shape[1]
    near, far = lax.axis_size(NEAR), lax.axis_size(FAR)

    own = half_weights(out_proj)
    attended = attend_block(queries, cache_keys, cache_values, new_keys, new_values, lengths)
    arrived = project(attended, own)
    choices = jnp.concatenate([expert_ids, gate_levels], axis=1).astype(jnp.bfloat16)
    choices = jnp.pad(choices, ((0, 0), (0, LANES - 2 * top_k)))
    whole = pl.BlockSpec(memory_space=pltpu.VMEM)
    residual, sent = pl.pallas_call(
        norm_kernel,
        out_shape=(
            jax.ShapeDtypeStruct((tokens, width), jnp.float32),
            jax.ShapeDtypeStruct((tokens, width + LANES), jnp.bfloat16),
        ),
        in_specs=[whole] * 4,
        out_specs=(whole, whole),
    )(
        *held(
            pltpu.VMEM,
            arrived.reshape([lax.axis_size(name) for name in SUMS_TO] + list(arrived.shape[1:])),
        ),
        hidden,
        norm_gain.reshape(1, width),
        choices,
    )

    pool = [sent] + [shift(sent, NEAR, by) for by in range(1, near)]
    outgoing, scaled = pick_rows(pool, width, top_k)
    incoming = swap(outgoing.reshape(far, SLOTS, width), FAR).reshape(far * SLOTS, width)
    half_out = expert_rows(incoming, expert_gate, expert_up, expert_down)
    returned = swap(half_out.reshape(far, SLOTS, width), FAR).reshape(far * SLOTS, width)
    mixed = lax.dot_general(
        scaled, returned, (((0,), (0,)), ((), ())), preferred_element_type=jnp.float32
    ).astype(jnp.bfloat16)
    parts = [mixed[:tokens]] + [
        shift(mixed[by * tokens : (by + 1) * tokens], NEAR, -by) for by in range(1, near)
    ]
    mixture = sum(part.astype(jnp.float32) for part in parts)
    return (residual + mixture).astype(jnp.bfloat16)


def solution(mesh):
    fine = Mesh(mesh.devices.reshape(2, 2, 4, 4, 2, 2), AXES)
    token = EXPERT + ("head",)
    placed = (
        P(token, None),
        P(EXPERT, "head", None),
        P(EXPERT, None, "head", None),
        P(EXPERT, None, "head", None),
        P(EXPERT, "head", None),
        P(EXPERT, "head", None),
        P(EXPERT),
        P("head", DEV),
        P(),
        P(EXPERT, None, "head"),
        P(EXPERT, None, "head"),
        P(EXPERT, "head", None),
        P(token, None),
        P(token, None),
    )
    return jax.shard_map(
        on_device,
        mesh=fine,
        in_specs=placed,
        out_specs=P(token, None),
        check_vma=False,
    )
```

```python
import math

import jax
import jax.numpy as jnp
from jax import lax
from jax.experimental import pallas as pl
from jax.experimental.pallas import tpu as pltpu
from jax.sharding import Mesh
from jax.sharding import PartitionSpec as P

AXES = ("role", "xh", "y", "zq", "zp", "head")
DEV = ("xh", "y", "zq", "zp")
EXPERT = ("role",) + DEV
RING = ("zq", "zp")
ROWS_FROM = ("role", "xh", "y")
SUMS_TO = ("role", "xh", "y", "head")
NEAR = "zq"
FAR = ("xh", "head", "y", "zp", "role")
CAP = 2
BLOCK = 8
SLOTS = 8
LANES = 128
RING_COST = 5 * 10**9


def attend_kernel(
    queries_ref, keys_ref, values_ref, new_keys_ref, new_values_ref, lengths_ref, out_ref,
    scores, blended
):
    requests, columns, size = keys_ref.shape
    heads = queries_ref.shape[1]
    kv_heads = new_keys_ref.shape[1]
    group = heads // kv_heads
    scaling = 1.0 / math.sqrt(size)
    for request in range(requests):
        scores[request] = lax.dot_general(
            queries_ref[request],
            keys_ref[request],
            (((1,), (1,)), ((), ())),
            preferred_element_type=jnp.float32,
        )
    row = lax.broadcasted_iota(jnp.int32, (heads, columns), 0)
    column = lax.broadcasted_iota(jnp.int32, (heads, columns), 1)
    own = row // group == column % kv_heads
    position = column // kv_heads
    first = lax.broadcasted_iota(jnp.int32, (heads, size), 0) < group

    def of_head(pair_ref, request):
        pair = pair_ref[request].astype(jnp.float32)
        return jnp.where(first, pair[0:1], pair[1:2])

    for request in range(requests):
        query = queries_ref[request].astype(jnp.float32)
        latest = jnp.sum(query * of_head(new_keys_ref, request), axis=1, keepdims=True) * scaling
        usable = own & (position < lengths_ref[request])
        masked = jnp.where(usable, scores[request] * scaling, -1e30)
        highest = jnp.maximum(jnp.max(masked, axis=1, keepdims=True), latest)
        terms = jnp.exp(masked - highest)
        newest = jnp.exp(latest - highest)
        total = jnp.sum(terms, axis=1, keepdims=True) + newest
        weights = (terms / total).astype(jnp.bfloat16)
        weight = (newest / total).astype(jnp.bfloat16).astype(jnp.float32)
        blend = jnp.dot(weights, values_ref[request], preferred_element_type=jnp.float32)
        blend = blend + weight * of_head(new_values_ref, request)
        blended[request * heads : (request + 1) * heads, :] = blend
    roles, near, rows, _ = out_ref.shape
    for role in range(roles):
        for head in range(group):
            part = blended[pl.ds(role * group + head, rows, stride=heads), :]
            part = part.astype(jnp.bfloat16)
            for copy in range(near):
                out_ref[role, copy, :, head * LANES : (head + 1) * LANES] = part


def attend(queries, keys, values, new_keys, new_values, lengths, near):
    rows, heads, size = queries.shape
    positions, kv_heads = keys.shape[1:3]
    columns = positions * kv_heads
    whole = pl.BlockSpec(memory_space=pltpu.VMEM)
    return pl.pallas_call(
        attend_kernel,
        out_shape=jax.ShapeDtypeStruct(
            (kv_heads, near, rows, heads // kv_heads * size), jnp.bfloat16
        ),
        in_specs=[whole] * 5 + [pl.BlockSpec(memory_space=pltpu.SMEM)],
        out_specs=whole,
        scratch_shapes=[
            pltpu.VMEM((rows, heads, columns), jnp.float32),
            pltpu.VMEM((rows * heads, size), jnp.float32),
        ],
        compiler_params=pltpu.CompilerParams(vmem_limit_bytes=16 << 20),
    )(
        *held(
            pltpu.HBM,
            queries,
            keys.reshape(rows, columns, size),
            values.reshape(rows, columns, size),
            new_keys,
            new_values,
        ),
        lengths,
    )


def swap(blocks, axes):
    return lax.all_to_all(blocks, axes, split_axis=0, concat_axis=0, tiled=True)


def shift(block, axis, by):
    count = lax.axis_size(axis)
    return lax.ppermute(block, axis, [(at, (at + by) % count) for at in range(count)])


def held(memory, *arrays):
    return [pltpu.with_memory_space_constraint(array, memory) for array in arrays]


def join_kernel(top_ref, bottom_ref, out_ref):
    part = top_ref.shape[0]
    out_ref[:part, :] = top_ref[...]
    out_ref[part:, :] = bottom_ref[...]


def project_kernel(spots, at_ref, rows_ref, *refs):
    pieces, out_ref, weights = refs[:-2], refs[-2], refs[-1]
    width = pieces[0].shape[0]
    count = weights.shape[0] // width
    for (by, first), piece_ref in zip(spots, pieces):
        place = lax.rem(at_ref[0] - by + count, count) * width + first
        to = pl.ds(pl.multiple_of(place, width // 2), piece_ref.shape[0])
        weights[to, :] = piece_ref[...]
    out_ref[...] = lax.dot_general(
        rows_ref[...], weights[...], (((1,), (1,)), ((), ())), preferred_element_type=jnp.float32
    ).astype(jnp.bfloat16)


def norm_kernel(arrived_ref, hidden_ref, gain_ref, choices_ref, residual_ref, sent_ref):
    roles, halves, rings, heads, tokens, width = arrived_ref.shape
    rows = width // LANES
    total = jnp.zeros((tokens, LANES), jnp.float32)
    for x in range(halves):
        for y in range(rings):
            for z in range(rows):
                span = slice(z * LANES, (z + 1) * LANES)
                first = (x * rings + y) * width + z * LANES
                to = slice(first, first + LANES)
                value = hidden_ref[:, to].astype(jnp.float32)
                for r in range(roles):
                    for h in range(heads):
                        value = value + arrived_ref[r, x, y, h, :, span].astype(jnp.float32)
                residual_ref[:, to] = value
                total = total + value * value
    count = residual_ref.shape[1]
    scale = lax.rsqrt(jnp.sum(total, axis=1, keepdims=True) / count + 1e-06)
    sent_ref[:, :count] = (residual_ref[...] * scale * gain_ref[...]).astype(jnp.bfloat16)
    sent_ref[:, count:] = choices_ref[...]


def pick_kernel(top_k, blocks, quad_ref, *refs):
    choices_refs, pool_refs = refs[:blocks], refs[blocks : 2 * blocks]
    out_ref, scaled_ref, picks = refs[2 * blocks :]
    count, tokens = picks.shape

    @pl.when(pl.program_id(0) == 0)
    def _():
        table = jnp.concatenate([ref[...].astype(jnp.float32) for ref in choices_refs], axis=0).T
        slot = lax.broadcasted_iota(jnp.int32, (count, tokens), 0)
        token = lax.broadcasted_iota(jnp.int32, (count, tokens), 1)
        far = slot // SLOTS
        chip = far // 32 * 4 + far // 4 % 4
        expert = far % 2 * 64 + chip * 8 + quad_ref[0] * 2 + far // 2 % 2
        expert = expert.astype(jnp.float32)
        levels = table[top_k : 2 * top_k]
        shares = levels / jnp.sum(levels, axis=0, keepdims=True)
        named = jnp.zeros((count, tokens), jnp.float32)
        share = jnp.zeros((count, tokens), jnp.float32)
        for at in range(top_k):
            hit = table[at : at + 1] == expert
            named = named + jnp.where(hit, 1.0, 0.0)
            share = share + jnp.where(hit, shares[at : at + 1], 0.0)
        row = lax.broadcasted_iota(jnp.int32, (tokens, tokens), 0)
        col = lax.broadcasted_iota(jnp.int32, (tokens, tokens), 1)
        before = jnp.where((row // BLOCK == col // BLOCK) & (row < col), 1.0, 0.0)
        earlier = jnp.dot(
            named.astype(jnp.bfloat16),
            before.astype(jnp.bfloat16),
            preferred_element_type=jnp.float32,
        )
        rank = (slot % CAP).astype(jnp.float32)
        chosen = (named > 0) & (earlier == rank) & (token // BLOCK == slot % SLOTS // CAP)
        scaled_ref[...] = jnp.where(chosen, share, 0.0).astype(jnp.bfloat16)
        picks[...] = jnp.where(chosen, 1.0, 0.0).astype(jnp.bfloat16)

    pool = jnp.concatenate([ref[...] for ref in pool_refs], axis=0)
    out_ref[...] = jnp.dot(picks[...], pool, preferred_element_type=jnp.float32).astype(
        jnp.bfloat16
    )


def pick_rows(pool, width, top_k):
    blocks, rows = len(pool), pool[0].shape[0]
    tokens = blocks * rows
    count = lax.axis_size(FAR) * SLOTS
    block = 1024
    quad = lax.axis_index("zq").astype(jnp.int32).reshape(1)
    return pl.pallas_call(
        lambda *refs: pick_kernel(top_k, blocks, *refs),
        out_shape=(
            jax.ShapeDtypeStruct((count, width), jnp.bfloat16),
            jax.ShapeDtypeStruct((count, tokens), jnp.bfloat16),
        ),
        grid=(width // block,),
        in_specs=[pl.BlockSpec(memory_space=pltpu.SMEM)]
        + [pl.BlockSpec((rows, LANES), lambda s: (0, width // LANES))] * blocks
        + [pl.BlockSpec((rows, block), lambda s: (0, s))] * blocks,
        out_specs=(
            pl.BlockSpec((count, block), lambda s: (0, s)),
            pl.BlockSpec((count, tokens), lambda s: (0, 0)),
        ),
        scratch_shapes=[pltpu.VMEM((count, tokens), jnp.bfloat16)],
        compiler_params=pltpu.CompilerParams(
            dimension_semantics=("arbitrary",), vmem_limit_bytes=16 << 20
        ),
    )(quad, *held(pltpu.HBM, pool[0]), *pool[1:], *held(pltpu.HBM, pool[0]), *pool[1:])


def ffn_kernel(unit_steps, rows_ref, gate_ref, up_ref, down_hbm, out_ref, active, down_ref, arrival):
    step = pl.program_id(0)
    fetch = pltpu.make_async_copy(down_hbm, down_ref, arrival)

    @pl.when(step == 0)
    def _():
        fetch.start()

    @pl.when(step == unit_steps)
    def _():
        fetch.wait()

    @pl.when(step < unit_steps)
    def _():
        to = pl.ds(pl.multiple_of(step * LANES, LANES), LANES)
        both = jnp.dot(
            rows_ref[...],
            jnp.concatenate([gate_ref[0, :, to], up_ref[0, :, to]], axis=1),
            preferred_element_type=jnp.float32,
        )
        gated = jax.nn.silu(both[:, :LANES]) * both[:, LANES:]
        active[:, to] = gated.astype(jnp.bfloat16)

    @pl.when(step >= unit_steps)
    def _():
        columns = out_ref.shape[1]
        first = jnp.maximum(step - unit_steps, 0) * columns
        out_ref[...] = jnp.dot(
            active[...],
            down_ref[0, :, pl.ds(pl.multiple_of(first, columns), columns)],
            preferred_element_type=jnp.float32,
        ).astype(jnp.bfloat16)


def expert_rows(rows, gate, up, down):
    count, width = rows.shape
    units = gate.shape[2]
    columns = 1024
    steps = units // LANES
    whole = pl.BlockSpec(memory_space=pltpu.VMEM)
    return pl.pallas_call(
        lambda *refs: ffn_kernel(steps, *refs),
        out_shape=jax.ShapeDtypeStruct((count, width), jnp.bfloat16),
        grid=(steps + width // columns,),
        in_specs=[whole] * 3 + [pl.BlockSpec(memory_space=pl.ANY)],
        out_specs=pl.BlockSpec((count, columns), lambda s: (0, jnp.maximum(s - steps, 0))),
        scratch_shapes=[
            pltpu.VMEM((count, units), jnp.bfloat16),
            pltpu.VMEM(down.shape, jnp.bfloat16),
            pltpu.SemaphoreType.DMA,
        ],
        compiler_params=pltpu.CompilerParams(
            dimension_semantics=("arbitrary",), vmem_limit_bytes=16 << 20
        ),
        cost_estimate=pl.CostEstimate(
            flops=6 * count * width * units,
            bytes_accessed=2 * (2 * count * width + 3 * width * units),
            transcendentals=count * units,
        ),
    )(*held(pltpu.VMEM, rows, gate, up), *held(pltpu.HBM, down))


def half_weights(out_proj):
    half = out_proj.shape[0] // 2
    return lax.dynamic_slice_in_dim(out_proj.T, lax.axis_index("role") * half, half, axis=1)


def project(sent, own):
    roles, near, rows, half = sent.shape
    ring, cols = lax.axis_size(RING), own.shape[0]
    up, down = shift(own, RING, 1), shift(own, RING, -1)
    whole = pl.BlockSpec(memory_space=pltpu.VMEM)
    sent, up, down = lax.optimization_barrier((sent, up, down))
    pieces, spots = [own, up, down], [(0, 0), (1, 0), (-1, 0)]
    gathered = swap(sent.reshape(roles * near, rows, half), ROWS_FROM)
    gathered = gathered.reshape(roles * near * rows, half)
    for by in range(2, ring // 2):
        up, down = shift(up, RING, 1), shift(down, RING, -1)
        pieces, spots = pieces + [up, down], spots + [(by, 0), (-by, 0)]
    part = cols // 2
    last = shift(up[:part], RING, 1), shift(down[part:], RING, -1)
    across = pl.pallas_call(
        join_kernel,
        out_shape=jax.ShapeDtypeStruct(own.shape, jnp.bfloat16),
        grid=(1,),
        in_specs=[whole, whole],
        out_specs=pl.BlockSpec(own.shape, lambda s: (0, 0)),
        cost_estimate=pl.CostEstimate(flops=RING_COST, bytes_accessed=0, transcendentals=0),
    )(*held(pltpu.VMEM, *last))
    pieces, spots = pieces + [across], spots + [(ring // 2, 0)]
    columns = pl.pallas_call(
        lambda *refs: project_kernel(spots, *refs),
        out_shape=jax.ShapeDtypeStruct((roles * near * rows, ring * cols), jnp.bfloat16),
        grid=(1,),
        in_specs=[pl.BlockSpec(memory_space=pltpu.SMEM)] + [whole] * (len(pieces) + 1),
        out_specs=pl.BlockSpec((roles * near * rows, ring * cols), lambda s: (0, 0)),
        scratch_shapes=[pltpu.VMEM((ring * cols, half), jnp.bfloat16)],
    )(lax.axis_index(RING).astype(jnp.int32).reshape(1), *held(pltpu.VMEM, gathered, *pieces))
    return swap(columns.reshape(2 * roles * near, rows // 2, ring * cols), SUMS_TO)


def on_device(
    hidden,
    queries,
    cache_keys,
    cache_values,
    new_keys,
    new_values,
    lengths,
    out_proj,
    norm_gain,
    expert_gate,
    expert_up,
    expert_down,
    expert_ids,
    gate_levels,
):
    tokens, width = hidden.shape
    top_k = expert_ids.shape[1]
    near, far = lax.axis_size(NEAR), lax.axis_size(FAR)

    own = half_weights(out_proj)
    copies = lax.axis_size("xh") * lax.axis_size("y")
    sent = attend(queries, cache_keys, cache_values, new_keys, new_values, lengths, copies)
    arrived = project(sent, own)
    choices = jnp.concatenate([expert_ids, gate_levels], axis=1).astype(jnp.bfloat16)
    choices = jnp.pad(choices, ((0, 0), (0, LANES - 2 * top_k)))
    whole = pl.BlockSpec(memory_space=pltpu.VMEM)
    residual, sent = pl.pallas_call(
        norm_kernel,
        out_shape=(
            jax.ShapeDtypeStruct((tokens, width), jnp.float32),
            jax.ShapeDtypeStruct((tokens, width + LANES), jnp.bfloat16),
        ),
        in_specs=[whole] * 4,
        out_specs=(whole, whole),
    )(
        *held(
            pltpu.VMEM,
            arrived.reshape([lax.axis_size(name) for name in SUMS_TO] + list(arrived.shape[1:])),
        ),
        hidden,
        norm_gain.reshape(1, width),
        choices,
    )

    pool = [sent] + [shift(sent, NEAR, by) for by in range(1, near)]
    outgoing, scaled = pick_rows(pool, width, top_k)
    incoming = swap(outgoing.reshape(far, SLOTS, width), FAR).reshape(far * SLOTS, width)
    half_out = expert_rows(incoming, expert_gate, expert_up, expert_down)
    returned = swap(half_out.reshape(far, SLOTS, width), FAR).reshape(far * SLOTS, width)
    mixed = lax.dot_general(
        scaled, returned, (((0,), (0,)), ((), ())), preferred_element_type=jnp.float32
    ).astype(jnp.bfloat16)
    parts = [mixed[:tokens]] + [
        shift(mixed[by * tokens : (by + 1) * tokens], NEAR, -by) for by in range(1, near)
    ]
    mixture = sum(part.astype(jnp.float32) for part in parts)
    return (residual + mixture).astype(jnp.bfloat16)


def solution(mesh):
    fine = Mesh(mesh.devices.reshape(2, 2, 4, 4, 2, 2), AXES)
    token = EXPERT + ("head",)
    placed = (
        P(token, None),
        P(EXPERT, "head", None),
        P(EXPERT, None, "head", None),
        P(EXPERT, None, "head", None),
        P(EXPERT, "head", None),
        P(EXPERT, "head", None),
        P(EXPERT),
        P("head", DEV),
        P(),
        P(EXPERT, None, "head"),
        P(EXPERT, None, "head"),
        P(EXPERT, "head", None),
        P(token, None),
        P(token, None),
    )
    return jax.shard_map(
        on_device,
        mesh=fine,
        in_specs=placed,
        out_specs=P(token, None),
        check_vma=False,
    )
```

```python
import math

import jax
import jax.numpy as jnp
from jax import lax
from jax.experimental import pallas as pl
from jax.experimental.pallas import tpu as pltpu
from jax.sharding import Mesh
from jax.sharding import PartitionSpec as P

AXES = ("role", "xh", "y", "zq", "zp", "head")
DEV = ("xh", "y", "zq", "zp")
EXPERT = ("role",) + DEV
RING = ("zq", "zp")
ROWS_FROM = ("role", "xh", "y")
SUMS_TO = ("role", "xh", "y", "head")
NEAR = "zq"
FAR = ("xh", "head", "y", "zp", "role")
CAP = 2
BLOCK = 8
SLOTS = 8
LANES = 128
RING_COST = 5 * 10**9


def attend_kernel(
    queries_ref, keys_ref, values_ref, new_keys_ref, new_values_ref, lengths_ref, out_ref,
    scores, blended
):
    requests, columns, size = keys_ref.shape
    heads = queries_ref.shape[1]
    kv_heads = new_keys_ref.shape[1]
    group = heads // kv_heads
    scaling = 1.0 / math.sqrt(size)
    for request in range(requests):
        scores[request] = lax.dot_general(
            queries_ref[request],
            keys_ref[request],
            (((1,), (1,)), ((), ())),
            preferred_element_type=jnp.float32,
        )
    row = lax.broadcasted_iota(jnp.int32, (heads, columns), 0)
    column = lax.broadcasted_iota(jnp.int32, (heads, columns), 1)
    own = row // group == column % kv_heads
    position = column // kv_heads
    first = lax.broadcasted_iota(jnp.int32, (heads, size), 0) < group

    def of_head(pair_ref, request):
        pair = pair_ref[request].astype(jnp.float32)
        return jnp.where(first, pair[0:1], pair[1:2])

    for request in range(requests):
        query = queries_ref[request].astype(jnp.float32)
        latest = jnp.sum(query * of_head(new_keys_ref, request), axis=1, keepdims=True) * scaling
        usable = own & (position < lengths_ref[request])
        masked = jnp.where(usable, scores[request] * scaling, -1e30)
        highest = jnp.maximum(jnp.max(masked, axis=1, keepdims=True), latest)
        terms = jnp.exp(masked - highest)
        newest = jnp.exp(latest - highest)
        total = jnp.sum(terms, axis=1, keepdims=True) + newest
        weights = (terms / total).astype(jnp.bfloat16)
        weight = (newest / total).astype(jnp.bfloat16).astype(jnp.float32)
        blend = jnp.dot(weights, values_ref[request], preferred_element_type=jnp.float32)
        blend = blend + weight * of_head(new_values_ref, request)
        blended[request * heads : (request + 1) * heads, :] = blend
    roles, near, rows, _ = out_ref.shape
    for role in range(roles):
        for head in range(group):
            part = blended[pl.ds(role * group + head, rows, stride=heads), :]
            part = part.astype(jnp.bfloat16)
            for copy in range(near):
                out_ref[role, copy, :, head * LANES : (head + 1) * LANES] = part


def attend(queries, keys, values, new_keys, new_values, lengths, near):
    rows, heads, size = queries.shape
    positions, kv_heads = keys.shape[1:3]
    columns = positions * kv_heads
    whole = pl.BlockSpec(memory_space=pltpu.VMEM)
    return pl.pallas_call(
        attend_kernel,
        out_shape=jax.ShapeDtypeStruct(
            (kv_heads, near, rows, heads // kv_heads * size), jnp.bfloat16
        ),
        in_specs=[whole] * 5 + [pl.BlockSpec(memory_space=pltpu.SMEM)],
        out_specs=whole,
        scratch_shapes=[
            pltpu.VMEM((rows, heads, columns), jnp.float32),
            pltpu.VMEM((rows * heads, size), jnp.float32),
        ],
        compiler_params=pltpu.CompilerParams(vmem_limit_bytes=16 << 20),
    )(
        *held(
            pltpu.HBM,
            queries,
            keys.reshape(rows, columns, size),
            values.reshape(rows, columns, size),
            new_keys,
            new_values,
        ),
        lengths,
    )


def swap(blocks, axes):
    return lax.all_to_all(blocks, axes, split_axis=0, concat_axis=0, tiled=True)


def shift(block, axis, by):
    count = lax.axis_size(axis)
    return lax.ppermute(block, axis, [(at, (at + by) % count) for at in range(count)])


def held(memory, *arrays):
    return [pltpu.with_memory_space_constraint(array, memory) for array in arrays]


def token_kernel(top_ref, bottom_ref, out_ref):
    out_ref[...] = top_ref[:BLOCK, :LANES] + bottom_ref[:BLOCK, :LANES]


def project_kernel(spots, at_ref, _, rows_ref, *refs):
    pieces, out_ref, weights = refs[:-2], refs[-2], refs[-1]
    width = pieces[0].shape[0]
    count = weights.shape[0] // width
    for (by, first), piece_ref in zip(spots, pieces):
        place = lax.rem(at_ref[0] - by + count, count) * width + first
        to = pl.ds(pl.multiple_of(place, width // 2), piece_ref.shape[0])
        weights[to, :] = piece_ref[...]
    out_ref[...] = lax.dot_general(
        rows_ref[...], weights[...], (((1,), (1,)), ((), ())), preferred_element_type=jnp.float32
    ).astype(jnp.bfloat16)


def norm_kernel(arrived_ref, hidden_ref, gain_ref, choices_ref, residual_ref, sent_ref):
    roles, halves, rings, heads, tokens, width = arrived_ref.shape
    rows = width // LANES
    total = jnp.zeros((tokens, LANES), jnp.float32)
    for x in range(halves):
        for y in range(rings):
            for z in range(rows):
                span = slice(z * LANES, (z + 1) * LANES)
                first = (x * rings + y) * width + z * LANES
                to = slice(first, first + LANES)
                value = hidden_ref[:, to].astype(jnp.float32)
                for r in range(roles):
                    for h in range(heads):
                        value = value + arrived_ref[r, x, y, h, :, span].astype(jnp.float32)
                residual_ref[:, to] = value
                total = total + value * value
    count = residual_ref.shape[1]
    scale = lax.rsqrt(jnp.sum(total, axis=1, keepdims=True) / count + 1e-06)
    sent_ref[:, :count] = (residual_ref[...] * scale * gain_ref[...]).astype(jnp.bfloat16)
    sent_ref[:, count:] = choices_ref[...]


def pick_kernel(top_k, blocks, quad_ref, *refs):
    choices_refs, pool_refs = refs[:blocks], refs[blocks : 2 * blocks]
    out_ref, scaled_ref, picks = refs[2 * blocks :]
    count, tokens = picks.shape

    @pl.when(pl.program_id(0) == 0)
    def _():
        table = jnp.concatenate([ref[...].astype(jnp.float32) for ref in choices_refs], axis=0).T
        slot = lax.broadcasted_iota(jnp.int32, (count, tokens), 0)
        token = lax.broadcasted_iota(jnp.int32, (count, tokens), 1)
        far = slot // SLOTS
        chip = far // 32 * 4 + far // 4 % 4
        expert = far % 2 * 64 + chip * 8 + quad_ref[0] * 2 + far // 2 % 2
        expert = expert.astype(jnp.float32)
        levels = table[top_k : 2 * top_k]
        shares = levels / jnp.sum(levels, axis=0, keepdims=True)
        named = jnp.zeros((count, tokens), jnp.float32)
        share = jnp.zeros((count, tokens), jnp.float32)
        for at in range(top_k):
            hit = table[at : at + 1] == expert
            named = named + jnp.where(hit, 1.0, 0.0)
            share = share + jnp.where(hit, shares[at : at + 1], 0.0)
        row = lax.broadcasted_iota(jnp.int32, (tokens, tokens), 0)
        col = lax.broadcasted_iota(jnp.int32, (tokens, tokens), 1)
        before = jnp.where((row // BLOCK == col // BLOCK) & (row < col), 1.0, 0.0)
        earlier = jnp.dot(
            named.astype(jnp.bfloat16),
            before.astype(jnp.bfloat16),
            preferred_element_type=jnp.float32,
        )
        rank = (slot % CAP).astype(jnp.float32)
        chosen = (named > 0) & (earlier == rank) & (token // BLOCK == slot % SLOTS // CAP)
        scaled_ref[...] = jnp.where(chosen, share, 0.0).astype(jnp.bfloat16)
        picks[...] = jnp.where(chosen, 1.0, 0.0).astype(jnp.bfloat16)

    pool = jnp.concatenate([ref[...] for ref in pool_refs], axis=0)
    out_ref[...] = jnp.dot(picks[...], pool, preferred_element_type=jnp.float32).astype(
        jnp.bfloat16
    )


def pick_rows(pool, width, top_k):
    blocks, rows = len(pool), pool[0].shape[0]
    tokens = blocks * rows
    count = lax.axis_size(FAR) * SLOTS
    block = 1024
    quad = lax.axis_index("zq").astype(jnp.int32).reshape(1)
    return pl.pallas_call(
        lambda *refs: pick_kernel(top_k, blocks, *refs),
        out_shape=(
            jax.ShapeDtypeStruct((count, width), jnp.bfloat16),
            jax.ShapeDtypeStruct((count, tokens), jnp.bfloat16),
        ),
        grid=(width // block,),
        in_specs=[pl.BlockSpec(memory_space=pltpu.SMEM)]
        + [pl.BlockSpec((rows, LANES), lambda s: (0, width // LANES))] * blocks
        + [pl.BlockSpec((rows, block), lambda s: (0, s))] * blocks,
        out_specs=(
            pl.BlockSpec((count, block), lambda s: (0, s)),
            pl.BlockSpec((count, tokens), lambda s: (0, 0)),
        ),
        scratch_shapes=[pltpu.VMEM((count, tokens), jnp.bfloat16)],
        compiler_params=pltpu.CompilerParams(
            dimension_semantics=("arbitrary",), vmem_limit_bytes=16 << 20
        ),
    )(quad, *held(pltpu.HBM, pool[0]), *pool[1:], *held(pltpu.HBM, pool[0]), *pool[1:])


def ffn_kernel(unit_steps, rows_ref, gate_ref, up_ref, down_hbm, out_ref, active, down_ref, arrival):
    step = pl.program_id(0)
    fetch = pltpu.make_async_copy(down_hbm, down_ref, arrival)

    @pl.when(step == 0)
    def _():
        fetch.start()

    @pl.when(step == unit_steps)
    def _():
        fetch.wait()

    @pl.when(step < unit_steps)
    def _():
        to = pl.ds(pl.multiple_of(step * LANES, LANES), LANES)
        both = jnp.dot(
            rows_ref[...],
            jnp.concatenate([gate_ref[0, :, to], up_ref[0, :, to]], axis=1),
            preferred_element_type=jnp.float32,
        )
        gated = jax.nn.silu(both[:, :LANES]) * both[:, LANES:]
        active[:, to] = gated.astype(jnp.bfloat16)

    @pl.when(step >= unit_steps)
    def _():
        columns = out_ref.shape[1]
        first = jnp.maximum(step - unit_steps, 0) * columns
        out_ref[...] = jnp.dot(
            active[...],
            down_ref[0, :, pl.ds(pl.multiple_of(first, columns), columns)],
            preferred_element_type=jnp.float32,
        ).astype(jnp.bfloat16)


def expert_rows(rows, gate, up, down):
    count, width = rows.shape
    units = gate.shape[2]
    columns = 1024
    steps = units // LANES
    whole = pl.BlockSpec(memory_space=pltpu.VMEM)
    return pl.pallas_call(
        lambda *refs: ffn_kernel(steps, *refs),
        out_shape=jax.ShapeDtypeStruct((count, width), jnp.bfloat16),
        grid=(steps + width // columns,),
        in_specs=[whole] * 3 + [pl.BlockSpec(memory_space=pl.ANY)],
        out_specs=pl.BlockSpec((count, columns), lambda s: (0, jnp.maximum(s - steps, 0))),
        scratch_shapes=[
            pltpu.VMEM((count, units), jnp.bfloat16),
            pltpu.VMEM(down.shape, jnp.bfloat16),
            pltpu.SemaphoreType.DMA,
        ],
        compiler_params=pltpu.CompilerParams(
            dimension_semantics=("arbitrary",), vmem_limit_bytes=16 << 20
        ),
        cost_estimate=pl.CostEstimate(
            flops=6 * count * width * units,
            bytes_accessed=2 * (2 * count * width + 3 * width * units),
            transcendentals=count * units,
        ),
    )(*held(pltpu.VMEM, rows, gate, up), *held(pltpu.HBM, down))


def half_weights(out_proj):
    half = out_proj.shape[0] // 2
    return lax.dynamic_slice_in_dim(out_proj.T, lax.axis_index("role") * half, half, axis=1)


def project(sent, own, choices):
    roles, near, rows, half = sent.shape
    ring, cols = lax.axis_size(RING), own.shape[0]
    up, down = shift(own, RING, 1), shift(own, RING, -1)
    whole = pl.BlockSpec(memory_space=pltpu.VMEM)
    sent, up, down, choices = lax.optimization_barrier((sent, up, down, choices))
    pieces, spots = [own, up, down], [(0, 0), (1, 0), (-1, 0)]
    gathered = swap(sent.reshape(roles * near, rows, half), ROWS_FROM)
    gathered = gathered.reshape(roles * near * rows, half)
    for by in range(2, ring // 2):
        up, down = shift(up, RING, 1), shift(down, RING, -1)
        pieces, spots = pieces + [up, down], spots + [(by, 0), (-by, 0)]
    part = cols // 2
    last = shift(up[:part], RING, 1), shift(down[part:], RING, -1)
    pieces = pieces + list(last)
    spots = spots + [(ring // 2, 0), (ring // 2, part)]
    token = pl.pallas_call(
        token_kernel,
        out_shape=jax.ShapeDtypeStruct((BLOCK, LANES), jnp.bfloat16),
        in_specs=[whole, whole],
        out_specs=whole,
        cost_estimate=pl.CostEstimate(flops=RING_COST, bytes_accessed=0, transcendentals=0),
    )(*held(pltpu.VMEM, *last))
    columns = pl.pallas_call(
        lambda *refs: project_kernel(spots, *refs),
        out_shape=jax.ShapeDtypeStruct((roles * near * rows, ring * cols), jnp.bfloat16),
        grid=(1,),
        in_specs=[pl.BlockSpec(memory_space=pltpu.SMEM), pl.BlockSpec(memory_space=pl.ANY)]
        + [whole] * (len(pieces) + 1),
        out_specs=pl.BlockSpec((roles * near * rows, ring * cols), lambda s: (0, 0)),
        scratch_shapes=[pltpu.VMEM((ring * cols, half), jnp.bfloat16)],
    )(lax.axis_index(RING).astype(jnp.int32).reshape(1), token, *held(pltpu.VMEM, gathered, *pieces))
    return choices, swap(columns.reshape(2 * roles * near, rows // 2, ring * cols), SUMS_TO)


def on_device(
    hidden,
    queries,
    cache_keys,
    cache_values,
    new_keys,
    new_values,
    lengths,
    out_proj,
    norm_gain,
    expert_gate,
    expert_up,
    expert_down,
    expert_ids,
    gate_levels,
):
    tokens, width = hidden.shape
    top_k = expert_ids.shape[1]
    near, far = lax.axis_size(NEAR), lax.axis_size(FAR)

    own = half_weights(out_proj)
    copies = lax.axis_size("xh") * lax.axis_size("y")
    sent = attend(queries, cache_keys, cache_values, new_keys, new_values, lengths, copies)
    choices = jnp.concatenate([expert_ids, gate_levels], axis=1).astype(jnp.bfloat16)
    choices = jnp.pad(choices, ((0, 0), (0, LANES - 2 * top_k)))
    choices, arrived = project(sent, own, choices)
    whole = pl.BlockSpec(memory_space=pltpu.VMEM)
    residual, sent = pl.pallas_call(
        norm_kernel,
        out_shape=(
            jax.ShapeDtypeStruct((tokens, width), jnp.float32),
            jax.ShapeDtypeStruct((tokens, width + LANES), jnp.bfloat16),
        ),
        in_specs=[whole] * 4,
        out_specs=(whole, whole),
    )(
        *held(
            pltpu.VMEM,
            arrived.reshape([lax.axis_size(name) for name in SUMS_TO] + list(arrived.shape[1:])),
        ),
        hidden,
        norm_gain.reshape(1, width),
        choices,
    )

    places = sorted(range(1, near), key=lambda by: min(by, near - by))
    pool = [sent] + [shift(sent, NEAR, by) for by in places]
    outgoing, scaled = pick_rows(pool, width, top_k)
    incoming = swap(outgoing.reshape(far, SLOTS, width), FAR).reshape(far * SLOTS, width)
    half_out = expert_rows(incoming, expert_gate, expert_up, expert_down)
    returned = swap(half_out.reshape(far, SLOTS, width), FAR).reshape(far * SLOTS, width)
    mixed = lax.dot_general(
        scaled, returned, (((0,), (0,)), ((), ())), preferred_element_type=jnp.float32
    ).astype(jnp.bfloat16)
    parts = [mixed[:tokens]] + [
        shift(mixed[at * tokens : (at + 1) * tokens], NEAR, -places[at - 1])
        for at in range(near - 1, 0, -1)
    ]
    mixture = sum(part.astype(jnp.float32) for part in parts)
    return (residual + mixture).astype(jnp.bfloat16)


def solution(mesh):
    fine = Mesh(mesh.devices.reshape(2, 2, 4, 4, 2, 2), AXES)
    token = EXPERT + ("head",)
    placed = (
        P(token, None),
        P(EXPERT, "head", None),
        P(EXPERT, None, "head", None),
        P(EXPERT, None, "head", None),
        P(EXPERT, "head", None),
        P(EXPERT, "head", None),
        P(EXPERT),
        P("head", DEV),
        P(),
        P(EXPERT, None, "head"),
        P(EXPERT, None, "head"),
        P(EXPERT, "head", None),
        P(token, None),
        P(token, None),
    )
    return jax.shard_map(
        on_device,
        mesh=fine,
        in_specs=placed,
        out_specs=P(token, None),
        check_vma=False,
    )
```

```python
import math

import jax
import jax.numpy as jnp
from jax import lax
from jax.experimental import pallas as pl
from jax.experimental.pallas import tpu as pltpu
from jax.sharding import Mesh
from jax.sharding import PartitionSpec as P

AXES = ("role", "xh", "y", "zq", "zp", "head")
DEV = ("xh", "y", "zq", "zp")
EXPERT = ("role",) + DEV
RING = ("zq", "zp")
ROWS_FROM = ("role", "xh", "y")
SUMS_TO = ("role", "xh", "y", "head")
NEAR = "zq"
FAR = ("xh", "head", "y", "zp", "role")
CAP = 2
BLOCK = 8
SLOTS = 8
LANES = 128
RING_COST = 5 * 10**9


def attend_kernel(
    queries_ref, keys_ref, values_ref, new_keys_ref, new_values_ref, lengths_ref, out_ref,
    scores, blended
):
    requests, columns, size = keys_ref.shape
    heads = queries_ref.shape[1]
    kv_heads = new_keys_ref.shape[1]
    group = heads // kv_heads
    scaling = 1.0 / math.sqrt(size)
    for request in range(requests):
        scores[request] = lax.dot_general(
            queries_ref[request],
            keys_ref[request],
            (((1,), (1,)), ((), ())),
            preferred_element_type=jnp.float32,
        )
    row = lax.broadcasted_iota(jnp.int32, (heads, columns), 0)
    column = lax.broadcasted_iota(jnp.int32, (heads, columns), 1)
    own = row // group == column % kv_heads
    position = column // kv_heads
    first = lax.broadcasted_iota(jnp.int32, (heads, size), 0) < group

    def of_head(pair_ref, request):
        pair = pair_ref[request].astype(jnp.float32)
        return jnp.where(first, pair[0:1], pair[1:2])

    for request in range(requests):
        query = queries_ref[request].astype(jnp.float32)
        latest = jnp.sum(query * of_head(new_keys_ref, request), axis=1, keepdims=True) * scaling
        usable = own & (position < lengths_ref[request])
        masked = jnp.where(usable, scores[request] * scaling, -1e30)
        highest = jnp.maximum(jnp.max(masked, axis=1, keepdims=True), latest)
        terms = jnp.exp(masked - highest)
        newest = jnp.exp(latest - highest)
        total = jnp.sum(terms, axis=1, keepdims=True) + newest
        weights = (terms / total).astype(jnp.bfloat16)
        weight = (newest / total).astype(jnp.bfloat16).astype(jnp.float32)
        blend = jnp.dot(weights, values_ref[request], preferred_element_type=jnp.float32)
        blend = blend + weight * of_head(new_values_ref, request)
        blended[request * heads : (request + 1) * heads, :] = blend
    roles, near, rows, _ = out_ref.shape
    for role in range(roles):
        for head in range(group):
            part = blended[pl.ds(role * group + head, rows, stride=heads), :]
            part = part.astype(jnp.bfloat16)
            for copy in range(near):
                out_ref[role, copy, :, head * LANES : (head + 1) * LANES] = part


def attend(queries, keys, values, new_keys, new_values, lengths, near):
    rows, heads, size = queries.shape
    positions, kv_heads = keys.shape[1:3]
    columns = positions * kv_heads
    whole = pl.BlockSpec(memory_space=pltpu.VMEM)
    return pl.pallas_call(
        attend_kernel,
        out_shape=jax.ShapeDtypeStruct(
            (kv_heads, near, rows, heads // kv_heads * size), jnp.bfloat16
        ),
        in_specs=[whole] * 5 + [pl.BlockSpec(memory_space=pltpu.SMEM)],
        out_specs=whole,
        scratch_shapes=[
            pltpu.VMEM((rows, heads, columns), jnp.float32),
            pltpu.VMEM((rows * heads, size), jnp.float32),
        ],
        compiler_params=pltpu.CompilerParams(vmem_limit_bytes=16 << 20),
    )(
        *held(
            pltpu.HBM,
            queries,
            keys.reshape(rows, columns, size),
            values.reshape(rows, columns, size),
            new_keys,
            new_values,
        ),
        lengths,
    )


def swap(blocks, axes):
    return lax.all_to_all(blocks, axes, split_axis=0, concat_axis=0, tiled=True)


def shift(block, axis, by):
    count = lax.axis_size(axis)
    return lax.ppermute(block, axis, [(at, (at + by) % count) for at in range(count)])


def held(memory, *arrays):
    return [pltpu.with_memory_space_constraint(array, memory) for array in arrays]


def token_kernel(top_ref, bottom_ref, out_ref):
    out_ref[...] = top_ref[:BLOCK, :LANES] + bottom_ref[:BLOCK, :LANES]


def project_kernel(spots, at_ref, _, rows_ref, *refs):
    pieces, out_ref, weights = refs[:-2], refs[-2], refs[-1]
    width = pieces[0].shape[0]
    count = weights.shape[0] // width
    for (by, first), piece_ref in zip(spots, pieces):
        place = lax.rem(at_ref[0] - by + count, count) * width + first
        to = pl.ds(pl.multiple_of(place, width // 2), piece_ref.shape[0])
        weights[to, :] = piece_ref[...]
    out_ref[...] = lax.dot_general(
        rows_ref[...], weights[...], (((1,), (1,)), ((), ())), preferred_element_type=jnp.float32
    ).astype(jnp.bfloat16)


def norm_kernel(arrived_ref, hidden_ref, gain_ref, choices_ref, residual_ref, sent_ref):
    roles, halves, rings, heads, tokens, width = arrived_ref.shape
    rows = width // LANES
    total = jnp.zeros((tokens, LANES), jnp.float32)
    for x in range(halves):
        for y in range(rings):
            for z in range(rows):
                span = slice(z * LANES, (z + 1) * LANES)
                first = (x * rings + y) * width + z * LANES
                to = slice(first, first + LANES)
                value = hidden_ref[:, to].astype(jnp.float32)
                for r in range(roles):
                    for h in range(heads):
                        value = value + arrived_ref[r, x, y, h, :, span].astype(jnp.float32)
                residual_ref[:, to] = value
                total = total + value * value
    count = residual_ref.shape[1]
    scale = lax.rsqrt(jnp.sum(total, axis=1, keepdims=True) / count + 1e-06)
    sent_ref[:, :count] = (residual_ref[...] * scale * gain_ref[...]).astype(jnp.bfloat16)
    sent_ref[:, count:] = choices_ref[...]


def pick_kernel(top_k, blocks, quad_ref, *refs):
    pool_refs = refs[:blocks]
    out_ref, scaled_ref, picks = refs[blocks:]
    count, tokens = picks.shape
    block = out_ref.shape[1]
    width = pool_refs[0].shape[1] - LANES

    @pl.when(pl.program_id(0) == 0)
    def _():
        table = jnp.concatenate(
            [ref[:, width:].astype(jnp.float32) for ref in pool_refs], axis=0
        ).T
        slot = lax.broadcasted_iota(jnp.int32, (count, tokens), 0)
        token = lax.broadcasted_iota(jnp.int32, (count, tokens), 1)
        far = slot // SLOTS
        chip = far // 32 * 4 + far // 4 % 4
        expert = far % 2 * 64 + chip * 8 + quad_ref[0] * 2 + far // 2 % 2
        expert = expert.astype(jnp.float32)
        levels = table[top_k : 2 * top_k]
        shares = levels / jnp.sum(levels, axis=0, keepdims=True)
        named = jnp.zeros((count, tokens), jnp.float32)
        share = jnp.zeros((count, tokens), jnp.float32)
        for at in range(top_k):
            hit = table[at : at + 1] == expert
            named = named + jnp.where(hit, 1.0, 0.0)
            share = share + jnp.where(hit, shares[at : at + 1], 0.0)
        row = lax.broadcasted_iota(jnp.int32, (tokens, tokens), 0)
        col = lax.broadcasted_iota(jnp.int32, (tokens, tokens), 1)
        before = jnp.where((row // BLOCK == col // BLOCK) & (row < col), 1.0, 0.0)
        earlier = jnp.dot(
            named.astype(jnp.bfloat16),
            before.astype(jnp.bfloat16),
            preferred_element_type=jnp.float32,
        )
        rank = (slot % CAP).astype(jnp.float32)
        chosen = (named > 0) & (earlier == rank) & (token // BLOCK == slot % SLOTS // CAP)
        scaled_ref[...] = jnp.where(chosen, share, 0.0).astype(jnp.bfloat16)
        picks[...] = jnp.where(chosen, 1.0, 0.0).astype(jnp.bfloat16)

    span = pl.ds(pl.multiple_of(pl.program_id(0) * block, block), block)
    pool = jnp.concatenate([ref[:, span] for ref in pool_refs], axis=0)
    out_ref[...] = jnp.dot(picks[...], pool, preferred_element_type=jnp.float32).astype(
        jnp.bfloat16
    )


def pick_rows(pool, width, top_k):
    blocks, rows = len(pool), pool[0].shape[0]
    tokens = blocks * rows
    count = lax.axis_size(FAR) * SLOTS
    block = 1024
    quad = lax.axis_index("zq").astype(jnp.int32).reshape(1)
    return pl.pallas_call(
        lambda *refs: pick_kernel(top_k, blocks, *refs),
        out_shape=(
            jax.ShapeDtypeStruct((count, width), jnp.bfloat16),
            jax.ShapeDtypeStruct((count, tokens), jnp.bfloat16),
        ),
        grid=(width // block,),
        in_specs=[pl.BlockSpec(memory_space=pltpu.SMEM)]
        + [pl.BlockSpec(memory_space=pltpu.VMEM)] * blocks,
        out_specs=(
            pl.BlockSpec((count, block), lambda s: (0, s)),
            pl.BlockSpec((count, tokens), lambda s: (0, 0)),
        ),
        scratch_shapes=[pltpu.VMEM((count, tokens), jnp.bfloat16)],
        compiler_params=pltpu.CompilerParams(
            dimension_semantics=("arbitrary",), vmem_limit_bytes=16 << 20
        ),
    )(quad, *held(pltpu.VMEM, *pool))


def ffn_kernel(unit_steps, rows_ref, gate_ref, up_ref, down_hbm, out_ref, active, down_ref, arrival):
    step = pl.program_id(0)
    fetch = pltpu.make_async_copy(down_hbm, down_ref, arrival)

    @pl.when(step == 0)
    def _():
        fetch.start()

    @pl.when(step == unit_steps)
    def _():
        fetch.wait()

    @pl.when(step < unit_steps)
    def _():
        to = pl.ds(pl.multiple_of(step * LANES, LANES), LANES)
        both = jnp.dot(
            rows_ref[...],
            jnp.concatenate([gate_ref[0, :, to], up_ref[0, :, to]], axis=1),
            preferred_element_type=jnp.float32,
        )
        gated = jax.nn.silu(both[:, :LANES]) * both[:, LANES:]
        active[:, to] = gated.astype(jnp.bfloat16)

    @pl.when(step >= unit_steps)
    def _():
        columns = out_ref.shape[1]
        first = jnp.maximum(step - unit_steps, 0) * columns
        out_ref[...] = jnp.dot(
            active[...],
            down_ref[0, :, pl.ds(pl.multiple_of(first, columns), columns)],
            preferred_element_type=jnp.float32,
        ).astype(jnp.bfloat16)


def expert_rows(rows, gate, up, down):
    count, width = rows.shape
    units = gate.shape[2]
    columns = 2048
    steps = units // LANES
    whole = pl.BlockSpec(memory_space=pltpu.VMEM)
    return pl.pallas_call(
        lambda *refs: ffn_kernel(steps, *refs),
        out_shape=jax.ShapeDtypeStruct((count, width), jnp.bfloat16),
        grid=(steps + width // columns,),
        in_specs=[whole] * 3 + [pl.BlockSpec(memory_space=pl.ANY)],
        out_specs=pl.BlockSpec((count, columns), lambda s: (0, jnp.maximum(s - steps, 0))),
        scratch_shapes=[
            pltpu.VMEM((count, units), jnp.bfloat16),
            pltpu.VMEM(down.shape, jnp.bfloat16),
            pltpu.SemaphoreType.DMA,
        ],
        compiler_params=pltpu.CompilerParams(
            dimension_semantics=("arbitrary",), vmem_limit_bytes=16 << 20
        ),
        cost_estimate=pl.CostEstimate(
            flops=6 * count * width * units,
            bytes_accessed=2 * (2 * count * width + 3 * width * units),
            transcendentals=count * units,
        ),
    )(*held(pltpu.VMEM, rows, gate, up), *held(pltpu.HBM, down))


def half_weights(out_proj):
    half = out_proj.shape[0] // 2
    return lax.dynamic_slice_in_dim(out_proj.T, lax.axis_index("role") * half, half, axis=1)


def project(sent, own, choices):
    roles, near, rows, half = sent.shape
    ring, cols = lax.axis_size(RING), own.shape[0]
    up, down = shift(own, RING, 1), shift(own, RING, -1)
    whole = pl.BlockSpec(memory_space=pltpu.VMEM)
    sent, up, down, choices = lax.optimization_barrier((sent, up, down, choices))
    pieces, spots = [own, up, down], [(0, 0), (1, 0), (-1, 0)]
    gathered = swap(sent.reshape(roles * near, rows, half), ROWS_FROM)
    gathered = gathered.reshape(roles * near * rows, half)
    for by in range(2, ring // 2):
        up, down = shift(up, RING, 1), shift(down, RING, -1)
        pieces, spots = pieces + [up, down], spots + [(by, 0), (-by, 0)]
    part = cols // 2
    last = shift(up[:part], RING, 1), shift(down[part:], RING, -1)
    pieces = pieces + list(last)
    spots = spots + [(ring // 2, 0), (ring // 2, part)]
    token = pl.pallas_call(
        token_kernel,
        out_shape=jax.ShapeDtypeStruct((BLOCK, LANES), jnp.bfloat16),
        in_specs=[whole, whole],
        out_specs=whole,
        cost_estimate=pl.CostEstimate(flops=RING_COST, bytes_accessed=0, transcendentals=0),
    )(*held(pltpu.VMEM, *last))
    columns = pl.pallas_call(
        lambda *refs: project_kernel(spots, *refs),
        out_shape=jax.ShapeDtypeStruct((roles * near * rows, ring * cols), jnp.bfloat16),
        grid=(1,),
        in_specs=[pl.BlockSpec(memory_space=pltpu.SMEM), pl.BlockSpec(memory_space=pl.ANY)]
        + [whole] * (len(pieces) + 1),
        out_specs=pl.BlockSpec((roles * near * rows, ring * cols), lambda s: (0, 0)),
        scratch_shapes=[pltpu.VMEM((ring * cols, half), jnp.bfloat16)],
    )(lax.axis_index(RING).astype(jnp.int32).reshape(1), token, *held(pltpu.VMEM, gathered, *pieces))
    return choices, swap(columns.reshape(2 * roles * near, rows // 2, ring * cols), SUMS_TO)


def on_device(
    hidden,
    queries,
    cache_keys,
    cache_values,
    new_keys,
    new_values,
    lengths,
    out_proj,
    norm_gain,
    expert_gate,
    expert_up,
    expert_down,
    expert_ids,
    gate_levels,
):
    tokens, width = hidden.shape
    top_k = expert_ids.shape[1]
    near, far = lax.axis_size(NEAR), lax.axis_size(FAR)

    own = half_weights(out_proj)
    copies = lax.axis_size("xh") * lax.axis_size("y")
    sent = attend(queries, cache_keys, cache_values, new_keys, new_values, lengths, copies)
    choices = jnp.concatenate([expert_ids, gate_levels], axis=1).astype(jnp.bfloat16)
    choices = jnp.pad(choices, ((0, 0), (0, LANES - 2 * top_k)))
    choices, arrived = project(sent, own, choices)
    whole = pl.BlockSpec(memory_space=pltpu.VMEM)
    residual, sent = pl.pallas_call(
        norm_kernel,
        out_shape=(
            jax.ShapeDtypeStruct((tokens, width), jnp.float32),
            jax.ShapeDtypeStruct((tokens, width + LANES), jnp.bfloat16),
        ),
        in_specs=[whole] * 4,
        out_specs=(whole, whole),
    )(
        *held(
            pltpu.VMEM,
            arrived.reshape([lax.axis_size(name) for name in SUMS_TO] + list(arrived.shape[1:])),
        ),
        hidden,
        norm_gain.reshape(1, width),
        choices,
    )

    places = sorted(range(1, near), key=lambda by: min(by, near - by))
    pool = [sent] + [shift(sent, NEAR, by) for by in places]
    outgoing, scaled = pick_rows(pool, width, top_k)
    incoming = swap(outgoing.reshape(far, SLOTS, width), FAR).reshape(far * SLOTS, width)
    half_out = expert_rows(incoming, expert_gate, expert_up, expert_down)
    returned = swap(half_out.reshape(far, SLOTS, width), FAR).reshape(far * SLOTS, width)
    mixed = lax.dot_general(
        scaled, returned, (((0,), (0,)), ((), ())), preferred_element_type=jnp.float32
    ).astype(jnp.bfloat16)
    parts = [mixed[:tokens]] + [
        shift(mixed[at * tokens : (at + 1) * tokens], NEAR, -places[at - 1])
        for at in range(near - 1, 0, -1)
    ]
    mixture = sum(part.astype(jnp.float32) for part in parts)
    return (residual + mixture).astype(jnp.bfloat16)


def solution(mesh):
    fine = Mesh(mesh.devices.reshape(2, 2, 4, 4, 2, 2), AXES)
    token = EXPERT + ("head",)
    placed = (
        P(token, None),
        P(EXPERT, "head", None),
        P(EXPERT, None, "head", None),
        P(EXPERT, None, "head", None),
        P(EXPERT, "head", None),
        P(EXPERT, "head", None),
        P(EXPERT),
        P("head", DEV),
        P(),
        P(EXPERT, None, "head"),
        P(EXPERT, None, "head"),
        P(EXPERT, "head", None),
        P(token, None),
        P(token, None),
    )
    return jax.shard_map(
        on_device,
        mesh=fine,
        in_specs=placed,
        out_specs=P(token, None),
        check_vma=False,
    )
```
